32 devices in a mesh: tm: 4 (over y, core), space: 8 (over z, x).
Axes of the slice: x: 2, y: 2, z: 4, core: 2. Of those that a mesh axis runs over, the one named last changes fastest.
Arguments:
- observed: float32 [8, 48, 1440], P('tm', 'space'), may hold values from -8 to 8
- noise_var: float32 [8], replicated, may hold values from 0.05 to 1
- spectral_var: float32 [1440, 48], P('space'), may hold values from 0.2 to 5
- time_scale: float32 [1440, 48], P('space'), may hold values from 1.5 to 2
Outputs:
- smoothed: float32 [8, 48, 1440], P('tm', 'space')
The draws below stay inside these ranges and needn't reach their ends.
All inputs are finite; a program needn't handle non-finite values.
Results may differ from the reference program's by a relative error of at most 0.00007.
Values sent between devices are 32-bit elements; how exact they have to be, the bound alone decides.
A program may use at most 64 MiB of HBM per device.

```python
import math
import jax
import jax.numpy as jnp
from jax import lax

LON = 1440
LAT = 48
HOURS = 8


def level_of(rng, shape, pieces, least, high):
    def one(axis_at, shards_of):
        heights = jax.random.uniform(jax.random.fold_in(jax.random.fold_in(rng, 6), axis_at), (shards_of,), jnp.float32, least / len(pieces), high / len(pieces))
        return jnp.repeat(jnp.exp(heights), shape[axis_at] // shards_of).reshape((-1,) + (1,) * (len(shape) - axis_at - 1))

    gain = one(*pieces[0])
    for cut in pieces[1:]:
        gain = gain * one(*cut)
    return gain


def centred(key, extent, spread, bound, pieces=(), dtype=jnp.bfloat16):
    drawn = jax.random.normal(key, extent, jnp.float32) * spread
    if len(pieces) > 0:
        drawn = level_of(key, extent, pieces, -0.22, 0.18) * drawn
    return jnp.clip(drawn, min=-bound, max=bound).astype(dtype)


def setup_inputs(seed: int = 0) -> dict:
    arg_keys = jax.random.split(jax.random.key(seed), 5)
    return {
        "observed": centred(arg_keys[0], (HOURS, LAT, LON), 1.5, 8.0, ((0, 4), (1, 8)), jnp.float32),
        "noise_var": jnp.clip(jnp.exp(jax.random.uniform(arg_keys[1], (HOURS,), jnp.float32, math.log(0.05), math.log(1.0))), 0.05, 1.0),
        "spectral_var": jnp.clip(jnp.exp(math.log(5.0) - 3.218876 * jax.random.uniform(arg_keys[2], (LON, LAT), jnp.float32) ** level_of(arg_keys[2], (LON, LAT), ((0, 8),), -0.2, 0.2)), 0.2, 5.0),
        "time_scale": jnp.clip(jnp.exp(math.log(2.0) - 0.2876821 * jax.random.uniform(arg_keys[3], (LON, LAT), jnp.float32) ** level_of(arg_keys[3], (LON, LAT), ((0, 8),), -0.2, 0.2)), 1.5, 2.0),
    }


HIGHEST = lax.Precision.HIGHEST
ROOT_FIVE = 2.23606797749979
NILPOTENT = ((1.0, 1.0, 0.0), (0.0, 1.0, 1.0), (-1.0, -3.0, -2.0))
NILPOTENT_SQUARED = ((1.0, 2.0, 1.0), (-1.0, -2.0, -1.0), (1.0, 2.0, 1.0))
STATIONARY = ((1.0, 0.0, -1.0 / 3.0), (0.0, 1.0 / 3.0, 0.0), (-1.0 / 3.0, 0.0, 1.0))

def lon_basis(size):
    mode_index = lax.broadcasted_iota(jnp.int32, (size, size), 0)
    longitude = lax.broadcasted_iota(jnp.int32, (size, size), 1)
    half_size = size // 2
    sine_rows = mode_index > half_size
    frequency = jnp.where(sine_rows, mode_index - half_size, mode_index)
    radians = (frequency * longitude % size).astype(jnp.float32) * (2.0 * math.pi / size)
    waveform = jnp.where(sine_rows, jnp.sin(radians), jnp.cos(radians))
    edge_rows = (mode_index == 0) | (mode_index == half_size)
    weight = jnp.where(edge_rows, math.sqrt(1.0 / size), math.sqrt(2.0 / size))
    return waveform * weight

def lat_basis(size):
    wavenumber = lax.broadcasted_iota(jnp.int32, (size, size), 0)
    latitude = lax.broadcasted_iota(jnp.int32, (size, size), 1)
    radians = (wavenumber * (2 * latitude + 1) % (4 * size)).astype(jnp.float32) * (math.pi / (2.0 * size))
    weight = jnp.where(wavenumber == 0, math.sqrt(1.0 / size), math.sqrt(2.0 / size))
    return jnp.cos(radians) * weight

def mat_mul(left, right):
    return [[left[across][0] * right[0][within] + left[across][1] * right[1][within] + left[across][2] * right[2][within] for within in range(3)] for across in range(3)]

def mat_vec(matrix, vector):
    return [matrix[across][0] * vector[0] + matrix[across][1] * vector[1] + matrix[across][2] * vector[2] for across in range(3)]

def transposed(matrix):
    return [[matrix[within][across] for within in range(3)] for across in range(3)]

def inverted(matrix):
    cofactor = [[matrix[1][1] * matrix[2][2] - matrix[1][2] * matrix[2][1], matrix[0][2] * matrix[2][1] - matrix[0][1] * matrix[2][2], matrix[0][1] * matrix[1][2] - matrix[0][2] * matrix[1][1]], [matrix[1][2] * matrix[2][0] - matrix[1][0] * matrix[2][2], matrix[0][0] * matrix[2][2] - matrix[0][2] * matrix[2][0], matrix[0][2] * matrix[1][0] - matrix[0][0] * matrix[1][2]], [matrix[1][0] * matrix[2][1] - matrix[1][1] * matrix[2][0], matrix[0][1] * matrix[2][0] - matrix[0][0] * matrix[2][1], matrix[0][0] * matrix[1][1] - matrix[0][1] * matrix[1][0]]]
    determinant = matrix[0][0] * cofactor[0][0] + matrix[0][1] * cofactor[1][0] + matrix[0][2] * cofactor[2][0]
    return [[cofactor[across][within] / determinant for within in range(3)] for across in range(3)]

def model_terms(variance, scale):
    decay_rate = ROOT_FIVE / scale
    damping = jnp.exp(-decay_rate)
    transition = [[damping * ((1.0 if across == within else 0.0) + decay_rate * NILPOTENT[across][within] + 0.5 * decay_rate * decay_rate * NILPOTENT_SQUARED[across][within]) for within in range(3)] for across in range(3)]
    stationary = [[variance * STATIONARY[across][within] for within in range(3)] for across in range(3)]
    carried = mat_mul(mat_mul(transition, stationary), transposed(transition))
    process_noise = [[stationary[across][within] - carried[across][within] for within in range(3)] for across in range(3)]
    return (transition, stationary, process_noise)

def predict_cov(covariance, transition, process_noise):
    carried = mat_mul(mat_mul(transition, covariance), transposed(transition))
    return [[carried[across][within] + process_noise[across][within] for within in range(3)] for across in range(3)]

def gain_and_cov(predicted_cov, noise):
    innovation_var = predicted_cov[0][0] + noise
    kalman_gain = [predicted_cov[across][0] / innovation_var for across in range(3)]
    covariance = [[predicted_cov[across][within] - kalman_gain[across] * predicted_cov[0][within] for within in range(3)] for across in range(3)]
    return (kalman_gain, covariance)

def smooth_series(spectra, noise_var, variance, scale):
    transition, stationary, process_noise = model_terms(variance, scale)
    zeros = jnp.zeros_like(variance)

    def forward(carry, inputs):
        mean_state, covariance = carry
        observed, noise = inputs
        predicted_cov = predict_cov(covariance, transition, process_noise)
        smoother_gain = mat_mul(mat_mul(covariance, transposed(transition)), inverted(predicted_cov))
        predicted = mat_vec(transition, mean_state)
        kalman_gain, covariance = gain_and_cov(predicted_cov, noise)
        residual = observed - predicted[0]
        mean_state = [predicted[across] + kalman_gain[across] * residual for across in range(3)]
        return ((mean_state, covariance), (mean_state, smoother_gain))
    _, (means, gains) = lax.scan(forward, ([zeros, zeros, zeros], stationary), (spectra, noise_var))

    def backward(later, inputs):
        mean_state, smoother_gain = inputs
        projected = mat_vec(transition, mean_state)
        difference = [later[across] - projected[across] for across in range(3)]
        correction = mat_vec(smoother_gain, difference)
        smoothed_state = [mean_state[across] + correction[across] for across in range(3)]
        return (smoothed_state, smoothed_state[0])
    last_state = [means[across][-1] for across in range(3)]
    earlier_means = [means[across][:-1] for across in range(3)]
    next_gains = [[gains[across][within][1:] for within in range(3)] for across in range(3)]
    _, field = lax.scan(backward, last_state, (earlier_means, next_gains), reverse=True)
    return jnp.concatenate([field, last_state[0][None]], axis=0)

def reference(observed, noise_var, spectral_var, time_scale):
    lon_table = lon_basis(LON)
    lat_table = lat_basis(LAT)
    spectra = jnp.einsum('hal,jl->hja', observed, lon_table, precision=HIGHEST)
    spectra = jnp.einsum('hja,na->hjn', spectra, lat_table, precision=HIGHEST)
    blocks = 16
    shaped = spectra.reshape(HOURS, blocks, LON // blocks, LAT).transpose(1, 0, 2, 3)
    variances = spectral_var.reshape(blocks, LON // blocks, LAT)
    scales = time_scale.reshape(blocks, LON // blocks, LAT)

    def per_block(bundle):
        series, variance, scale = bundle
        return smooth_series(series, noise_var, variance, scale)
    smooth = lax.map(per_block, (shaped, variances, scales))
    smooth = smooth.transpose(1, 0, 2, 3).reshape(HOURS, LON, LAT)
    latitude_grid = jnp.einsum('hjn,na->hja', smooth, lat_table, precision=HIGHEST)
    return jnp.einsum('hja,jl->hal', latitude_grid, lon_table, precision=HIGHEST)
```

```python
import functools
import math

import jax
import jax.numpy as jnp
import numpy as np
from jax import lax
from jax.experimental import pallas as pl
from jax.experimental.pallas import tpu as pltpu
from jax.sharding import PartitionSpec as P

HIGHEST = lax.Precision.HIGHEST
ROOT_FIVE = 2.23606797749979
NILPOTENT = ((1.0, 1.0, 0.0), (0.0, 1.0, 1.0), (-1.0, -3.0, -2.0))
NILPOTENT_SQUARED = ((1.0, 2.0, 1.0), (-1.0, -2.0, -1.0), (1.0, 2.0, 1.0))
STATIONARY = ((1.0, 0.0, -1.0 / 3.0), (0.0, 1.0 / 3.0, 0.0), (-1.0 / 3.0, 0.0, 1.0))


def lon_basis(size):
    mode_index = lax.broadcasted_iota(jnp.int32, (size, size), 0)
    longitude = lax.broadcasted_iota(jnp.int32, (size, size), 1)
    half_size = size // 2
    sine_rows = mode_index > half_size
    frequency = jnp.where(sine_rows, mode_index - half_size, mode_index)
    radians = (frequency * longitude % size).astype(jnp.float32) * (2.0 * math.pi / size)
    waveform = jnp.where(sine_rows, jnp.sin(radians), jnp.cos(radians))
    edge_rows = (mode_index == 0) | (mode_index == half_size)
    weight = jnp.where(edge_rows, math.sqrt(1.0 / size), math.sqrt(2.0 / size))
    return waveform * weight


def lat_basis(size):
    wavenumber = lax.broadcasted_iota(jnp.int32, (size, size), 0)
    latitude = lax.broadcasted_iota(jnp.int32, (size, size), 1)
    radians = (wavenumber * (2 * latitude + 1) % (4 * size)).astype(jnp.float32) * (
        math.pi / (2.0 * size)
    )
    weight = jnp.where(wavenumber == 0, math.sqrt(1.0 / size), math.sqrt(2.0 / size))
    return jnp.cos(radians) * weight


def mat_mul(left, right):
    return [
        [
            left[across][0] * right[0][within]
            + left[across][1] * right[1][within]
            + left[across][2] * right[2][within]
            for within in range(3)
        ]
        for across in range(3)
    ]


def mat_vec(matrix, vector):
    return [
        matrix[across][0] * vector[0]
        + matrix[across][1] * vector[1]
        + matrix[across][2] * vector[2]
        for across in range(3)
    ]


def transposed(matrix):
    return [[matrix[within][across] for within in range(3)] for across in range(3)]


def inverted(matrix):
    cofactor = [
        [
            matrix[1][1] * matrix[2][2] - matrix[1][2] * matrix[2][1],
            matrix[0][2] * matrix[2][1] - matrix[0][1] * matrix[2][2],
            matrix[0][1] * matrix[1][2] - matrix[0][2] * matrix[1][1],
        ],
        [
            matrix[1][2] * matrix[2][0] - matrix[1][0] * matrix[2][2],
            matrix[0][0] * matrix[2][2] - matrix[0][2] * matrix[2][0],
            matrix[0][2] * matrix[1][0] - matrix[0][0] * matrix[1][2],
        ],
        [
            matrix[1][0] * matrix[2][1] - matrix[1][1] * matrix[2][0],
            matrix[0][1] * matrix[2][0] - matrix[0][0] * matrix[2][1],
            matrix[0][0] * matrix[1][1] - matrix[0][1] * matrix[1][0],
        ],
    ]
    determinant = (
        matrix[0][0] * cofactor[0][0]
        + matrix[0][1] * cofactor[1][0]
        + matrix[0][2] * cofactor[2][0]
    )
    return [[cofactor[across][within] / determinant for within in range(3)] for across in range(3)]


def model_terms(variance, scale):
    decay_rate = ROOT_FIVE / scale
    damping = jnp.exp(-decay_rate)
    transition = [
        [
            damping
            * (
                (1.0 if across == within else 0.0)
                + decay_rate * NILPOTENT[across][within]
                + 0.5 * decay_rate * decay_rate * NILPOTENT_SQUARED[across][within]
            )
            for within in range(3)
        ]
        for across in range(3)
    ]
    stationary = [
        [variance * STATIONARY[across][within] for within in range(3)] for across in range(3)
    ]
    carried = mat_mul(mat_mul(transition, stationary), transposed(transition))
    process_noise = [
        [stationary[across][within] - carried[across][within] for within in range(3)]
        for across in range(3)
    ]
    return (transition, stationary, process_noise)


def predict_cov(covariance, transition, process_noise):
    carried = mat_mul(mat_mul(transition, covariance), transposed(transition))
    return [
        [carried[across][within] + process_noise[across][within] for within in range(3)]
        for across in range(3)
    ]


def gain_and_cov(predicted_cov, noise):
    innovation_var = predicted_cov[0][0] + noise
    kalman_gain = [predicted_cov[across][0] / innovation_var for across in range(3)]
    covariance = [
        [
            predicted_cov[across][within] - kalman_gain[across] * predicted_cov[0][within]
            for within in range(3)
        ]
        for across in range(3)
    ]
    return (kalman_gain, covariance)


def smooth_series(spectra, noise_var, variance, scale):
    transition, stationary, process_noise = model_terms(variance, scale)
    zeros = jnp.zeros_like(variance)

    def forward(carry, inputs):
        mean_state, covariance = carry
        observed, noise = inputs
        predicted_cov = predict_cov(covariance, transition, process_noise)
        smoother_gain = mat_mul(
            mat_mul(covariance, transposed(transition)), inverted(predicted_cov)
        )
        predicted = mat_vec(transition, mean_state)
        kalman_gain, covariance = gain_and_cov(predicted_cov, noise)
        residual = observed - predicted[0]
        mean_state = [predicted[across] + kalman_gain[across] * residual for across in range(3)]
        return ((mean_state, covariance), (mean_state, smoother_gain))

    _, (means, gains) = lax.scan(forward, ([zeros, zeros, zeros], stationary), (spectra, noise_var))

    def backward(later, inputs):
        mean_state, smoother_gain = inputs
        projected = mat_vec(transition, mean_state)
        difference = [later[across] - projected[across] for across in range(3)]
        correction = mat_vec(smoother_gain, difference)
        smoothed_state = [mean_state[across] + correction[across] for across in range(3)]
        return (smoothed_state, smoothed_state[0])

    last_state = [means[across][-1] for across in range(3)]
    earlier_means = [means[across][:-1] for across in range(3)]
    next_gains = [[gains[across][within][1:] for within in range(3)] for across in range(3)]
    _, field = lax.scan(backward, last_state, (earlier_means, next_gains), reverse=True)
    return jnp.concatenate([field, last_state[0][None]], axis=0)


def per_device_general(observed, noise_var, spectral_var, time_scale):
    hours_dev, lat_dev, lon_size = observed.shape
    band_count = lax.axis_size("space")
    lat_size = lat_dev * band_count
    modes_dev = lon_size // band_count
    lon_table = lon_basis(lon_size)
    lat_table = lat_basis(lat_size).reshape(lat_size, band_count, lat_dev)
    grid_rows = observed.reshape(hours_dev * lat_dev, lon_size)
    spectra = lax.dot_general(lon_table, grid_rows, (((1,), (1,)), ((), ())), precision=HIGHEST)
    by_mode = lax.all_to_all(spectra, "space", split_axis=0, concat_axis=1, tiled=True)
    by_mode = by_mode.reshape(modes_dev, band_count, hours_dev, lat_dev)
    coefficients = jnp.einsum("msha,nsa->hmn", by_mode, lat_table, precision=HIGHEST)
    flat = coefficients.reshape(hours_dev, modes_dev * lat_size)
    hourly = lax.all_to_all(flat, "tm", split_axis=1, concat_axis=0, tiled=True)
    share = flat.shape[1] // lax.axis_size("tm")
    offset = lax.axis_index("tm") * share
    variance = lax.dynamic_slice_in_dim(spectral_var.reshape(-1), offset, share)
    scale = lax.dynamic_slice_in_dim(time_scale.reshape(-1), offset, share)
    series = smooth_series(hourly, noise_var, variance, scale)
    smooth = lax.all_to_all(series, "tm", split_axis=0, concat_axis=1, tiled=True).reshape(
        hours_dev, modes_dev, lat_size
    )
    latitude_grid = jnp.einsum("hmn,nsa->msha", smooth, lat_table, precision=HIGHEST)
    latitude_grid = latitude_grid.reshape(modes_dev, band_count * hours_dev * lat_dev)
    by_band = lax.all_to_all(latitude_grid, "space", split_axis=1, concat_axis=0, tiled=True)
    field = lax.dot_general(by_band, lon_table, (((0,), (0,)), ((), ())), precision=HIGHEST)
    return field.reshape(hours_dev, lat_dev, lon_size)


LANES = 128
ROWS = 8
MESH = pl.DeviceIdType.MESH
NT = (((1,), (1,)), ((), ()))
NN = (((1,), (0,)), ((), ()))


def round_up(value, unit):
    return -(-value // unit) * unit


KINDS = 3
WIDTH = LANES // 2
QUARTER = LANES // 4


def hops(time, band, times, bands):
    wide = math.isqrt(bands // 2)
    return time // 2 + band // wide + band % wide


def plan(times, bands):
    cosines = bands // 2
    jobs = [
        (band, kind)
        for base in (0, cosines)
        for kind in range(KINDS)
        for band in range(base, base + cosines)
    ]
    devices = [(time, band) for time in range(times) for band in range(bands)]
    chosen = sorted(devices, key=lambda d: (hops(*d, times, bands), d))[: len(jobs)]
    owner, free = {}, []
    for band in range(bands):
        local = sorted(d for d in chosen if d[1] == band)
        for kind, device in enumerate(local[:KINDS]):
            owner[band, kind] = device
        free.extend(local[KINDS:])
    free.sort(key=lambda d: -hops(*d, times, bands))
    sources, used = {}, {}
    for job in jobs:
        if job not in owner:
            owner[job] = free.pop(0)
            sources[job] = (used.get(job[0], 0), job[0])
            used[job[0]] = sources[job][0] + 1
    return jobs, [owner[job] for job in jobs], [sources.get(job) for job in jobs]


def mode_columns(modes_dev):
    full = modes_dev // KINDS
    return full, modes_dev // 2 - full


def lon_tables(lon_size, bands):
    half, cosines = lon_size // 2, bands // 2
    modes_dev = lon_size // bands
    full, rest = mode_columns(modes_dev)
    points = lon_size // 4 + 1
    padded = round_up(points, LANES)
    tables = np.zeros((4, cosines * (WIDTH + QUARTER), padded), np.float64)

    def fill(kind, column, mode):
        frequency = mode - half if mode > half else mode
        radians = (frequency * np.arange(points) % lon_size) * (2.0 * math.pi / lon_size)
        wave = np.sin(radians) if mode > half else np.cos(radians)
        wave = wave * math.sqrt((1.0 if mode in (0, half) else 2.0) / lon_size)
        wave[-1] *= 0.5
        tables[kind, column, :points] = wave

    for band in range(bands):
        for parity in range(2):
            kind = 2 * (band // cosines) + parity
            for index in range(full + rest):
                mode = band * modes_dev + 2 * index + parity
                local = band % cosines
                if index < full:
                    column = local * WIDTH + index
                else:
                    column = cosines * WIDTH + local * QUARTER + index - full
                if mode == half:
                    fill(0, WIDTH - 1, mode)
                else:
                    fill(kind, column, mode)
    tables = tables.astype(np.float32)
    high = tables.astype(jnp.bfloat16)
    low = (tables - high.astype(np.float32)).astype(jnp.bfloat16)
    return high, low


def lat_tables(lat_size, bands):
    lat_dev = lat_size // bands
    wavenumber = np.arange(lat_size)[:, None]
    latitude = np.arange(lat_size)[None, :]
    radians = (wavenumber * (2 * latitude + 1) % (4 * lat_size)) * (math.pi / (2.0 * lat_size))
    table = np.cos(radians) * np.where(wavenumber == 0, math.sqrt(1.0 / lat_size), math.sqrt(2.0 / lat_size))
    full = np.zeros((lat_size, bands, ROWS), np.float32)
    full[:, :, :lat_dev] = table.reshape(lat_size, bands, lat_dev)
    full = full.reshape(lat_size, bands * ROWS)

    def stacked(array):
        high = array.astype(jnp.bfloat16)
        return np.concatenate([high, (array - high.astype(np.float32)).astype(jnp.bfloat16)], axis=0)

    return stacked(full), stacked(np.ascontiguousarray(full.T))


def split(value):
    high = value.astype(jnp.bfloat16)
    low = (value - high.astype(jnp.float32)).astype(jnp.bfloat16)
    return high, low


def paired_dot(table, value):
    both = jnp.concatenate(split(value), axis=1)
    product = lax.dot_general(table, both, NN, preferred_element_type=jnp.float32)
    rows = table.shape[0] // 2
    return product[:rows, :LANES] + (product[:rows, LANES:] + product[rows:, :LANES])


def swap_halves(first, second):
    left = lax.broadcasted_iota(jnp.int32, first.shape, 1) < LANES // 2
    return (
        jnp.where(left, first, pltpu.roll(second, LANES // 2, 1)),
        jnp.where(left, pltpu.roll(first, LANES // 2, 1), second),
    )


def symmetric_gains(noise_ref, variance, scale, transition_ref, gain_ref, smoother_ref):
    hours = gain_ref.shape[0]
    transition, stationary, process = model_terms(variance, scale)
    pairs = [(0, 0), (0, 1), (0, 2), (1, 1), (1, 2), (2, 2)]
    for row in range(3):
        for column in range(3):
            transition_ref[row, column] = transition[row][column]

    def unpack(packed):
        matrix = [[None] * 3 for _ in range(3)]
        for (row, column), value in zip(pairs, packed):
            matrix[row][column] = matrix[column][row] = value
        return matrix

    def update(predicted, hour):
        inverse_var = 1.0 / (predicted[0][0] + noise_ref[hour])
        gain = [predicted[row][0] * inverse_var for row in range(3)]
        for row in range(3):
            gain_ref[hour, row] = gain[row]
        return [predicted[row][column] - gain[row] * predicted[0][column] for row, column in pairs]

    def step(hour, packed):
        covariance = unpack(packed)
        moved = mat_mul(transition, covariance)
        predicted = unpack(
            [
                moved[row][0] * transition[column][0]
                + moved[row][1] * transition[column][1]
                + moved[row][2] * transition[column][2]
                + process[row][column]
                for row, column in pairs
            ]
        )
        c00 = predicted[1][1] * predicted[2][2] - predicted[1][2] * predicted[1][2]
        c01 = predicted[0][2] * predicted[1][2] - predicted[0][1] * predicted[2][2]
        c02 = predicted[0][1] * predicted[1][2] - predicted[0][2] * predicted[1][1]
        c11 = predicted[0][0] * predicted[2][2] - predicted[0][2] * predicted[0][2]
        c12 = predicted[0][1] * predicted[0][2] - predicted[0][0] * predicted[1][2]
        c22 = predicted[0][0] * predicted[1][1] - predicted[0][1] * predicted[0][1]
        inverse_det = 1.0 / (predicted[0][0] * c00 + predicted[0][1] * c01 + predicted[0][2] * c02)
        cofactors = unpack([c00, c01, c02, c11, c12, c22])
        for row in range(3):
            scaled = [moved[within][row] * inverse_det for within in range(3)]
            for column in range(3):
                smoother_ref[hour - 1, row, column] = (
                    scaled[0] * cofactors[0][column]
                    + scaled[1] * cofactors[1][column]
                    + scaled[2] * cofactors[2][column]
                )
        return tuple(update(predicted, hour))

    first = tuple(update(stationary, 0))
    lax.fori_loop(1, hours, step, first)


def smoother_kernel(
    times,
    bands,
    observed_hbm,
    noise_hbm,
    variance_hbm,
    scale_hbm,
    forward_lat_hbm,
    inverse_lat_hbm,
    high_hbm,
    low_hbm,
    out_ref,
    observed_ref,
    noise_ref,
    variance_ref,
    scale_ref,
    forward_lat_ref,
    inverse_lat_ref,
    high,
    low,
    folded,
    outbox,
    inbox,
    outbox_back,
    inbox_back,
    params_out,
    params,
    transition_ref,
    gain_ref,
    smoother_ref,
    input_sem,
    table_sem,
    send_sem,
    recv_sem,
    send_back_sem,
    recv_back_sem,
    params_send_sem,
    params_recv_sem,
):
    devices = times * bands
    cosines = bands // 2
    stride = 5 if devices % 5 else 1
    jobs, owners, sources = plan(times, bands)
    codes = [time * bands + band for time, band in owners]
    my_time = lax.axis_index("tm")
    my_band = lax.axis_index("space")
    me = my_time * bands + my_band
    lat_dev, lon_size = observed_ref.shape[0], observed_ref.shape[2]
    half = lon_size // 2
    hours = gain_ref.shape[0]
    n_half = gain_ref.shape[2]
    modes_dev = variance_ref.shape[1]
    full, rest = mode_columns(modes_dev)
    points = high.shape[2]
    mirror = half % LANES

    def pick(index, values):
        total = 0
        for place, value in enumerate(values):
            total = total + jnp.where(index == place, value, 0)
        return total

    def mine(places, values):
        total = 0
        for place, value in zip(places, values):
            total = total + jnp.where(me == place, value, 0)
        return total

    my_job = mine(codes, range(1, len(jobs) + 1)) - 1
    owning = my_job >= 0
    moved = [index for index, source in enumerate(sources) if source is not None]
    source_codes = [sources[index][0] * bands + sources[index][1] for index in moved]
    lending = mine(source_codes, [1] * len(moved)) > 0
    borrowing = mine([codes[index] for index in moved], [1] * len(moved)) > 0

    def table_copy(kind, which):
        source, target = ((high_hbm, high), (low_hbm, low))[which]
        return pltpu.make_async_copy(source.at[kind], target.at[kind], table_sem.at[kind, which])

    inputs = [
        pltpu.make_async_copy(source, target, input_sem.at[index])
        for index, (source, target) in enumerate(
            [
                (observed_hbm, observed_ref),
                (variance_hbm, variance_ref),
                (scale_hbm, scale_ref),
                (noise_hbm, noise_ref),
                (forward_lat_hbm, forward_lat_ref),
                (inverse_lat_hbm, inverse_lat_ref),
            ]
        )
    ]
    inputs[0].start()
    inbox[...] = jnp.zeros_like(inbox)
    inbox_back[...] = jnp.zeros_like(inbox_back)

    barrier = pltpu.get_barrier_semaphore()

    @pl.when(owning)
    def _():
        def greet(step, carry):
            peer = lax.rem(me + step, devices)
            pl.semaphore_signal(
                barrier, inc=1, device_id=(peer // bands, lax.rem(peer, bands)), device_id_type=MESH
            )
            return carry

        lax.fori_loop(1, devices, greet, 0)

    for kind in range(4):
        table_copy(kind, 0).start()
        table_copy(kind, 1).start()
    for copy in inputs[1:]:
        copy.start()

    def own_modes(ref, kind):
        mode = lax.broadcasted_iota(jnp.int32, (modes_dev, LANES), 0)
        slot = lax.rem(lax.broadcasted_iota(jnp.int32, (modes_dev, LANES), 1), WIDTH)
        second = (slot >= QUARTER).astype(jnp.int32)
        place = slot - second * QUARTER
        whole = jnp.where(slot < full, 2 * slot + kind, modes_dev)
        mixed = jnp.where(place < rest, 2 * (full + place) + second, modes_dev)
        wanted = jnp.where(kind == KINDS - 1, mixed, whole)
        picked = (mode == wanted).astype(jnp.float32)
        lane = lax.broadcasted_iota(jnp.int32, (n_half, LANES), 1)
        used = wanted[:n_half] < modes_dev
        value = lax.dot_general(ref[...], picked, NN, precision=HIGHEST, preferred_element_type=jnp.float32)
        value = jnp.where(lane < WIDTH, value[:n_half], value[n_half:])
        return jnp.where(used, value, 1.0)

    folded[...] = jnp.zeros_like(folded)
    inputs[0].wait()
    lane = lax.broadcasted_iota(jnp.int32, (ROWS, LANES), 1)
    reverse = lax.rem(mirror + LANES - lane, LANES)
    straight = lane <= mirror

    def flipped(value):
        return jnp.take_along_axis(value, reverse, axis=1, mode="promise_in_bounds")

    def tile(value, index):
        return value[:, index * LANES : (index + 1) * LANES]

    last = half // LANES
    classes = [[], [], [], []]
    for hour in range(2):
        early = observed_ref[:, hour, :half]
        late = observed_ref[:, hour, half:]
        folded[0, hour, :lat_dev, :half] = early + late
        folded[1, hour, :lat_dev, :half] = early - late
        for parity in range(2):
            ahead = folded[parity, hour]
            turned = {index: flipped(tile(ahead, index)) for index in range(last - points // LANES, last + 1)}
            behind = jnp.concatenate(
                [
                    jnp.where(straight, turned[last - index], turned[last - index - 1])
                    for index in range(points // LANES)
                ],
                axis=1,
            )
            ahead = ahead[:, :points]
            classes[parity].append(ahead + behind if parity == 0 else ahead - behind)
            classes[2 + parity].append(ahead - behind if parity == 0 else ahead + behind)

    wide_lanes = cosines * WIDTH

    def forward(kind):
        table_copy(kind, 0).wait()
        table_copy(kind, 1).wait()
        upper, lower = split(jnp.concatenate(classes[kind], axis=0))
        both = jnp.concatenate([upper, lower], axis=0)
        wide = lax.dot_general(both, high[kind], NT, preferred_element_type=jnp.float32)
        fine = lax.dot_general(upper, low[kind], NT, preferred_element_type=jnp.float32)
        return wide[: 2 * ROWS] + wide[2 * ROWS :] + fine

    def spin(value, amount):
        amount = amount % LANES
        return pltpu.roll(value, amount, 1) if amount else value

    quarter = lane // QUARTER
    middle = None
    for side in range(2):
        found = [forward(2 * side), forward(2 * side + 1)]
        base = side * KINDS * cosines
        for parity in range(2):
            for pair in range(cosines // 2):
                block = tile(found[parity], pair)
                first, second = swap_halves(block[:ROWS], block[ROWS:])
                if side == 0 and parity == 0 and pair == 0:
                    middle = spin(first, 1)
                if side == 1 and parity == 0 and pair == 0:
                    first = jnp.where(lax.rem(lane, WIDTH) == 0, pltpu.roll(middle, WIDTH, 1), first)
                outbox[base + parity * cosines + 2 * pair] = first
                outbox[base + parity * cosines + 2 * pair + 1] = second
        mixed = [value[:, wide_lanes:] for value in found]
        for local in range(cosines):
            parts = [
                spin(mixed[part % 2][(part // 2) * ROWS : (part // 2 + 1) * ROWS], (part - local) * QUARTER)
                for part in range(4)
            ]
            merged = jnp.where(quarter == 0, parts[0], parts[1])
            merged = jnp.where(quarter == 2, parts[2], merged)
            outbox[base + 2 * cosines + local] = jnp.where(quarter == 3, parts[3], merged)

    inputs[1].wait()
    inputs[2].wait()

    @pl.when(lending)
    def _():
        kind = mine(source_codes, [jobs[index][1] for index in moved])
        params_out[0] = own_modes(variance_ref, kind)
        params_out[1] = own_modes(scale_ref, kind)

    @pl.when(owning)
    def _():
        kind = mine(codes, [kind for _, kind in jobs])

        @pl.when(jnp.logical_not(borrowing))
        def _():
            params[0] = own_modes(variance_ref, kind)
            params[1] = own_modes(scale_ref, kind)

    pl.semaphore_wait(barrier, len(jobs) - owning.astype(jnp.int32))

    def params_copy():
        target = mine(source_codes, [codes[index] for index in moved])
        return pltpu.make_async_remote_copy(
            src_ref=params_out,
            dst_ref=params,
            send_sem=params_send_sem.at[0],
            recv_sem=params_recv_sem.at[0],
            device_id=(target // bands, lax.rem(target, bands)),
            device_id_type=MESH,
        )

    @pl.when(lending)
    def _():
        params_copy().start()

    def exchange(box, landing, sends, recv, slot, peer, target):
        return pltpu.make_async_remote_copy(
            src_ref=box.at[slot, pl.ds(0, lat_dev)],
            dst_ref=landing.at[target, pl.ds(0, lat_dev)],
            send_sem=sends.at[0],
            recv_sem=recv,
            device_id=(peer // bands, lax.rem(peer, bands)),
            device_id_type=MESH,
        )

    def keep(box, landing, recv, slot, target):
        return pltpu.make_async_copy(
            box.at[slot, pl.ds(0, lat_dev)], landing.at[target, pl.ds(0, lat_dev)], recv
        )

    def landed(landing, recv, first, count):
        come = landing.at[pl.ds(first, count), pl.ds(0, lat_dev)]
        pltpu.make_async_copy(come, come, recv).wait()

    for group in range(2 * KINDS):
        for step in range(cosines):
            local = lax.rem(me + step, cosines)
            peer = pick(local, codes[group * cosines : (group + 1) * cosines])

            @pl.when(peer != me)
            def _():
                exchange(outbox, inbox, send_sem, recv_sem.at[my_time], group * cosines + local, peer, me).start()

    @pl.when(owning)
    def _():
        keep(outbox, inbox, recv_sem.at[my_time], my_job, me).start()

    for copy in inputs[3:]:
        copy.wait()

    @pl.when(owning)
    def _():
        @pl.when(borrowing)
        def _():
            pltpu.make_async_copy(params, params, params_recv_sem.at[0]).wait()

        symmetric_gains(noise_ref, params[0], params[1], transition_ref, gain_ref, smoother_ref)

        spectra = []
        for time in range(times):
            landed(inbox, recv_sem.at[time], time * bands, bands)
            arrived = inbox[time * bands : (time + 1) * bands].reshape(bands * ROWS, LANES)
            mixed = paired_dot(forward_lat_ref[...], arrived)
            spectra.extend(swap_halves(mixed[:n_half], mixed[n_half:]))

        transition = [[transition_ref[row, column] for column in range(3)] for row in range(3)]
        means, predictions = [], [None]
        means.append([gain_ref[0, row] * spectra[0] for row in range(3)])
        for hour in range(1, hours):
            predicted = mat_vec(transition, means[-1])
            residual = spectra[hour] - predicted[0]
            predictions.append(predicted)
            means.append([predicted[row] + gain_ref[hour, row] * residual for row in range(3)])
        smoothed = means[-1]
        series = [None] * hours
        series[hours - 1] = smoothed[0]
        for hour in range(hours - 2, -1, -1):
            difference = [smoothed[row] - predictions[hour + 1][row] for row in range(3)]
            smoothed = [
                means[hour][row]
                + smoother_ref[hour, row, 0] * difference[0]
                + smoother_ref[hour, row, 1] * difference[1]
                + smoother_ref[hour, row, 2] * difference[2]
                for row in range(3)
            ]
            series[hour] = smoothed[0]

        for time in range(times):
            stacked = jnp.concatenate(swap_halves(series[2 * time], series[2 * time + 1]), axis=0)
            grid = paired_dot(inverse_lat_ref[...], stacked)
            outbox_back[time * bands : (time + 1) * bands] = grid.reshape(bands, ROWS, LANES)

        def send_back(step, carry):
            peer = lax.rem(me + step * stride, devices)
            exchange(
                outbox_back, inbox_back, send_back_sem, recv_back_sem.at[my_job // cosines], peer, peer, my_job
            ).start()
            return carry

        lax.fori_loop(1, devices, send_back, 0)
        keep(outbox_back, inbox_back, recv_back_sem.at[my_job // cosines], me, my_job).start()

    sums = []
    later = None
    for side in range(2):
        base = side * KINDS * cosines
        boxes = {}
        for group in ((2, 0, 1) if side == 0 else (0, 2, 1)):
            landed(inbox_back, recv_back_sem.at[side * KINDS + group], base + group * cosines, cosines)
            for local in range(cosines):
                boxes[group, local] = inbox_back[base + group * cosines + local]
        shared = [[], []]
        for hour in range(2):
            for parity in range(2):
                merged = None
                for local in range(cosines):
                    moved_part = spin(boxes[2, local], (local - (2 * hour + parity)) * QUARTER)
                    merged = moved_part if merged is None else jnp.where(quarter == local, moved_part, merged)
                shared[parity].append(merged)
        for parity in range(2):
            blocks = []
            for pair in range(cosines // 2):
                first, second = swap_halves(boxes[parity, 2 * pair], boxes[parity, 2 * pair + 1])
                blocks.append([first, second])
            blocks.append(shared[parity])
            sums.append(blocks)
    origin = inbox_back[KINDS * cosines]
    for hour in range(2):
        shift = WIDTH - 1 - hour * WIDTH
        sums[0][0][hour] = jnp.where(lane == WIDTH - 1, spin(origin, shift), sums[0][0][hour])

    grids = []
    for kind in range(4):
        upper, lower = split(
            jnp.concatenate([jnp.concatenate(block, axis=0) for block in sums[kind]], axis=1)
        )
        both = jnp.concatenate([upper, lower], axis=0)
        wide = lax.dot_general(both, high[kind], NN, preferred_element_type=jnp.float32)
        fine = lax.dot_general(upper, low[kind], NN, preferred_element_type=jnp.float32)
        grids.append(wide[: 2 * ROWS] + wide[2 * ROWS :] + fine)

    count = points // LANES
    for hour in range(2):
        even_cos, odd_cos, even_sin, odd_sin = [grid[hour * ROWS : (hour + 1) * ROWS] for grid in grids]
        ahead, ahead_odd = even_cos + even_sin, odd_cos + odd_sin
        behind, behind_odd = even_cos - even_sin, odd_sin - odd_cos
        for side in range(2):
            start = ahead + ahead_odd if side == 0 else ahead - ahead_odd
            end = behind + behind_odd if side == 0 else behind - behind_odd
            turned = [flipped(tile(end, index)) for index in range(count)]
            pieces = [tile(start, index) for index in range(count - 1)]
            border = half // 2 - (count - 1) * LANES
            fold = tile(start, count - 1)
            fold = jnp.where(lane == border, fold + fold, fold)
            pieces.append(jnp.where(lane <= border, fold, turned[count - 1]))
            for index in range(count - 1, 0, -1):
                pieces.append(jnp.where(straight, turned[index], turned[index - 1]))
            pieces.append(turned[0])
            row = jnp.concatenate(pieces, axis=1)
            out_ref[:, hour, side * half : (side + 1) * half] = row[:lat_dev, :half]

    def gone(box, sends, count):
        left = box.at[pl.ds(0, count), pl.ds(0, lat_dev)]
        pltpu.make_async_copy(left, left, sends.at[0]).wait()

    gone(outbox, send_sem, len(jobs) - 1)

    @pl.when(jnp.logical_not(owning))
    def _():
        gone(outbox, send_sem, 1)

    @pl.when(owning)
    def _():
        gone(outbox_back, send_back_sem, devices - 1)

    @pl.when(lending)
    def _():
        pltpu.make_async_copy(params_out, params_out, params_send_sem.at[0]).wait()


def per_device_fused(observed, noise_var, spectral_var, time_scale):
    times, bands = lax.axis_size("tm"), lax.axis_size("space")
    hours_dev, lat_dev, lon_size = observed.shape
    hours, lat_size = noise_var.shape[0], spectral_var.shape[1]
    n_half = lat_size // 2
    half_padded = round_up(lon_size // 2, LANES)
    n_jobs = KINDS * bands

    high, low = lon_tables(lon_size, bands)
    forward_lat, inverse_lat = lat_tables(lat_size, bands)
    in_vmem = pl.BlockSpec(memory_space=pltpu.VMEM)
    in_place = pl.BlockSpec(memory_space=pltpu.HBM)
    box = pltpu.VMEM((times * bands, ROWS, LANES), jnp.float32)
    job_box = pltpu.VMEM((n_jobs, ROWS, LANES), jnp.float32)
    dma = pltpu.SemaphoreType.DMA
    field = pl.pallas_call(
        functools.partial(smoother_kernel, times, bands),
        out_shape=pltpu.VMEM((lat_dev, hours_dev, lon_size), jnp.float32),
        in_specs=[in_place] * 8,
        out_specs=in_vmem,
        scratch_shapes=[
            pltpu.VMEM((lat_dev, hours_dev, lon_size), jnp.float32),
            pltpu.SMEM((hours,), jnp.float32),
            pltpu.VMEM((lat_size, spectral_var.shape[0]), jnp.float32),
            pltpu.VMEM((lat_size, spectral_var.shape[0]), jnp.float32),
            pltpu.VMEM(forward_lat.shape, jnp.bfloat16),
            pltpu.VMEM(inverse_lat.shape, jnp.bfloat16),
            pltpu.VMEM(high.shape, jnp.bfloat16),
            pltpu.VMEM(low.shape, jnp.bfloat16),
            pltpu.VMEM((2, 2, ROWS, half_padded), jnp.float32),
            job_box,
            box,
            box,
            job_box,
            pltpu.VMEM((2, n_half, LANES), jnp.float32),
            pltpu.VMEM((2, n_half, LANES), jnp.float32),
            pltpu.VMEM((3, 3, n_half, LANES), jnp.float32),
            pltpu.VMEM((hours, 3, n_half, LANES), jnp.float32),
            pltpu.VMEM((hours, 3, 3, n_half, LANES), jnp.float32),
            dma((6,)),
            dma((4, 2)),
            dma((1,)),
            dma((times,)),
            dma((1,)),
            dma((2 * KINDS,)),
            dma((1,)),
            dma((1,)),
        ],
        compiler_params=pltpu.CompilerParams(collective_id=0, has_side_effects=True),
    )(
        observed.transpose(1, 0, 2),
        noise_var,
        spectral_var.T,
        time_scale.T,
        jnp.asarray(forward_lat),
        jnp.asarray(inverse_lat),
        jnp.asarray(high),
        jnp.asarray(low),
    )
    return field.transpose(1, 0, 2)


def fits(observed, spectral_var):
    times, bands = lax.axis_size("tm"), lax.axis_size("space")
    hours_dev, lat_dev, lon_size = observed.shape
    modes_dev, lat_size = spectral_var.shape
    full, rest = mode_columns(modes_dev)
    half, points = lon_size // 2, round_up(lon_size // 4 + 1, LANES)
    return (
        hours_dev == 2
        and lat_dev <= ROWS
        and lat_size % (2 * ROWS) == 0
        and times == KINDS + 1
        and 2 * math.isqrt(bands // 2) ** 2 == bands
        and bands == LANES // 16
        and lon_size % 4 == 0
        and modes_dev % 2 == 0
        and modes_dev % KINDS == 0
        and full < WIDTH
        and rest <= QUARTER
        and half % LANES > 0
        and round_up(half, LANES) == 2 * points
        and half // 2 >= points - LANES
    )


def per_device(observed, noise_var, spectral_var, time_scale):
    if fits(observed, spectral_var):
        return per_device_fused(observed, noise_var, spectral_var, time_scale)
    return per_device_general(observed, noise_var, spectral_var, time_scale)


def solution(mesh):
    placed = (P("tm", "space", None), P(), P("space", None), P("space", None))
    return jax.shard_map(
        per_device, mesh=mesh, in_specs=placed, out_specs=P("tm", "space", None), check_vma=False
    )
```

```python
import functools
import math

import jax
import jax.numpy as jnp
import numpy as np
from jax import lax
from jax.experimental import pallas as pl
from jax.experimental.pallas import tpu as pltpu
from jax.sharding import PartitionSpec as P

HIGHEST = lax.Precision.HIGHEST
ROOT_FIVE = 2.23606797749979
NILPOTENT = ((1.0, 1.0, 0.0), (0.0, 1.0, 1.0), (-1.0, -3.0, -2.0))
NILPOTENT_SQUARED = ((1.0, 2.0, 1.0), (-1.0, -2.0, -1.0), (1.0, 2.0, 1.0))
STATIONARY = ((1.0, 0.0, -1.0 / 3.0), (0.0, 1.0 / 3.0, 0.0), (-1.0 / 3.0, 0.0, 1.0))


def lon_basis(size):
    mode_index = lax.broadcasted_iota(jnp.int32, (size, size), 0)
    longitude = lax.broadcasted_iota(jnp.int32, (size, size), 1)
    half_size = size // 2
    sine_rows = mode_index > half_size
    frequency = jnp.where(sine_rows, mode_index - half_size, mode_index)
    radians = (frequency * longitude % size).astype(jnp.float32) * (2.0 * math.pi / size)
    waveform = jnp.where(sine_rows, jnp.sin(radians), jnp.cos(radians))
    edge_rows = (mode_index == 0) | (mode_index == half_size)
    weight = jnp.where(edge_rows, math.sqrt(1.0 / size), math.sqrt(2.0 / size))
    return waveform * weight


def lat_basis(size):
    wavenumber = lax.broadcasted_iota(jnp.int32, (size, size), 0)
    latitude = lax.broadcasted_iota(jnp.int32, (size, size), 1)
    radians = (wavenumber * (2 * latitude + 1) % (4 * size)).astype(jnp.float32) * (
        math.pi / (2.0 * size)
    )
    weight = jnp.where(wavenumber == 0, math.sqrt(1.0 / size), math.sqrt(2.0 / size))
    return jnp.cos(radians) * weight


def mat_mul(left, right):
    return [
        [
            left[across][0] * right[0][within]
            + left[across][1] * right[1][within]
            + left[across][2] * right[2][within]
            for within in range(3)
        ]
        for across in range(3)
    ]


def mat_vec(matrix, vector):
    return [
        matrix[across][0] * vector[0]
        + matrix[across][1] * vector[1]
        + matrix[across][2] * vector[2]
        for across in range(3)
    ]


def transposed(matrix):
    return [[matrix[within][across] for within in range(3)] for across in range(3)]


def inverted(matrix):
    cofactor = [
        [
            matrix[1][1] * matrix[2][2] - matrix[1][2] * matrix[2][1],
            matrix[0][2] * matrix[2][1] - matrix[0][1] * matrix[2][2],
            matrix[0][1] * matrix[1][2] - matrix[0][2] * matrix[1][1],
        ],
        [
            matrix[1][2] * matrix[2][0] - matrix[1][0] * matrix[2][2],
            matrix[0][0] * matrix[2][2] - matrix[0][2] * matrix[2][0],
            matrix[0][2] * matrix[1][0] - matrix[0][0] * matrix[1][2],
        ],
        [
            matrix[1][0] * matrix[2][1] - matrix[1][1] * matrix[2][0],
            matrix[0][1] * matrix[2][0] - matrix[0][0] * matrix[2][1],
            matrix[0][0] * matrix[1][1] - matrix[0][1] * matrix[1][0],
        ],
    ]
    determinant = (
        matrix[0][0] * cofactor[0][0]
        + matrix[0][1] * cofactor[1][0]
        + matrix[0][2] * cofactor[2][0]
    )
    return [[cofactor[across][within] / determinant for within in range(3)] for across in range(3)]


def model_terms(variance, scale):
    decay_rate = ROOT_FIVE / scale
    damping = jnp.exp(-decay_rate)
    transition = [
        [
            damping
            * (
                (1.0 if across == within else 0.0)
                + decay_rate * NILPOTENT[across][within]
                + 0.5 * decay_rate * decay_rate * NILPOTENT_SQUARED[across][within]
            )
            for within in range(3)
        ]
        for across in range(3)
    ]
    stationary = [
        [variance * STATIONARY[across][within] for within in range(3)] for across in range(3)
    ]
    carried = mat_mul(mat_mul(transition, stationary), transposed(transition))
    process_noise = [
        [stationary[across][within] - carried[across][within] for within in range(3)]
        for across in range(3)
    ]
    return (transition, stationary, process_noise)


def predict_cov(covariance, transition, process_noise):
    carried = mat_mul(mat_mul(transition, covariance), transposed(transition))
    return [
        [carried[across][within] + process_noise[across][within] for within in range(3)]
        for across in range(3)
    ]


def gain_and_cov(predicted_cov, noise):
    innovation_var = predicted_cov[0][0] + noise
    kalman_gain = [predicted_cov[across][0] / innovation_var for across in range(3)]
    covariance = [
        [
            predicted_cov[across][within] - kalman_gain[across] * predicted_cov[0][within]
            for within in range(3)
        ]
        for across in range(3)
    ]
    return (kalman_gain, covariance)


def smooth_series(spectra, noise_var, variance, scale):
    transition, stationary, process_noise = model_terms(variance, scale)
    zeros = jnp.zeros_like(variance)

    def forward(carry, inputs):
        mean_state, covariance = carry
        observed, noise = inputs
        predicted_cov = predict_cov(covariance, transition, process_noise)
        smoother_gain = mat_mul(
            mat_mul(covariance, transposed(transition)), inverted(predicted_cov)
        )
        predicted = mat_vec(transition, mean_state)
        kalman_gain, covariance = gain_and_cov(predicted_cov, noise)
        residual = observed - predicted[0]
        mean_state = [predicted[across] + kalman_gain[across] * residual for across in range(3)]
        return ((mean_state, covariance), (mean_state, smoother_gain))

    _, (means, gains) = lax.scan(forward, ([zeros, zeros, zeros], stationary), (spectra, noise_var))

    def backward(later, inputs):
        mean_state, smoother_gain = inputs
        projected = mat_vec(transition, mean_state)
        difference = [later[across] - projected[across] for across in range(3)]
        correction = mat_vec(smoother_gain, difference)
        smoothed_state = [mean_state[across] + correction[across] for across in range(3)]
        return (smoothed_state, smoothed_state[0])

    last_state = [means[across][-1] for across in range(3)]
    earlier_means = [means[across][:-1] for across in range(3)]
    next_gains = [[gains[across][within][1:] for within in range(3)] for across in range(3)]
    _, field = lax.scan(backward, last_state, (earlier_means, next_gains), reverse=True)
    return jnp.concatenate([field, last_state[0][None]], axis=0)


def per_device_general(observed, noise_var, spectral_var, time_scale):
    hours_dev, lat_dev, lon_size = observed.shape
    band_count = lax.axis_size("space")
    lat_size = lat_dev * band_count
    modes_dev = lon_size // band_count
    lon_table = lon_basis(lon_size)
    lat_table = lat_basis(lat_size).reshape(lat_size, band_count, lat_dev)
    grid_rows = observed.reshape(hours_dev * lat_dev, lon_size)
    spectra = lax.dot_general(lon_table, grid_rows, (((1,), (1,)), ((), ())), precision=HIGHEST)
    by_mode = lax.all_to_all(spectra, "space", split_axis=0, concat_axis=1, tiled=True)
    by_mode = by_mode.reshape(modes_dev, band_count, hours_dev, lat_dev)
    coefficients = jnp.einsum("msha,nsa->hmn", by_mode, lat_table, precision=HIGHEST)
    flat = coefficients.reshape(hours_dev, modes_dev * lat_size)
    hourly = lax.all_to_all(flat, "tm", split_axis=1, concat_axis=0, tiled=True)
    share = flat.shape[1] // lax.axis_size("tm")
    offset = lax.axis_index("tm") * share
    variance = lax.dynamic_slice_in_dim(spectral_var.reshape(-1), offset, share)
    scale = lax.dynamic_slice_in_dim(time_scale.reshape(-1), offset, share)
    series = smooth_series(hourly, noise_var, variance, scale)
    smooth = lax.all_to_all(series, "tm", split_axis=0, concat_axis=1, tiled=True).reshape(
        hours_dev, modes_dev, lat_size
    )
    latitude_grid = jnp.einsum("hmn,nsa->msha", smooth, lat_table, precision=HIGHEST)
    latitude_grid = latitude_grid.reshape(modes_dev, band_count * hours_dev * lat_dev)
    by_band = lax.all_to_all(latitude_grid, "space", split_axis=1, concat_axis=0, tiled=True)
    field = lax.dot_general(by_band, lon_table, (((0,), (0,)), ((), ())), precision=HIGHEST)
    return field.reshape(hours_dev, lat_dev, lon_size)


LANES = 128
ROWS = 8
MESH = pl.DeviceIdType.MESH
NT = (((1,), (1,)), ((), ()))
NN = (((1,), (0,)), ((), ()))


def round_up(value, unit):
    return -(-value // unit) * unit


KINDS = 3
WIDTH = LANES // 2
QUARTER = LANES // 4


def hops(time, band, times, bands):
    wide = math.isqrt(bands // 2)
    return time // 2 + band // wide + band % wide


def plan(times, bands):
    cosines = bands // 2
    jobs = [
        (band, kind)
        for base in (0, cosines)
        for kind in range(KINDS)
        for band in range(base, base + cosines)
    ]
    devices = [(time, band) for time in range(times) for band in range(bands)]
    chosen = sorted(devices, key=lambda d: (hops(*d, times, bands), d))[: len(jobs)]
    owner, sources, used = {}, {}, {}
    for side in range(2):
        pool = sorted(d for d in chosen if d[0] % 2 == side)
        wanted = [job for job in jobs if job[0] // cosines == side]
        for band in range(side * cosines, (side + 1) * cosines):
            for kind, device in enumerate([d for d in pool if d[1] == band][:KINDS]):
                owner[band, kind] = device
        taken = set(owner.values())
        free = sorted((d for d in pool if d not in taken), key=lambda d: -hops(*d, times, bands))
        for job in wanted:
            if job not in owner:
                owner[job] = free.pop(0)
                sources[job] = (used.get(job[0], 0), job[0])
                used[job[0]] = sources[job][0] + 1
    return jobs, [owner[job] for job in jobs], [sources.get(job) for job in jobs]


def balanced(times, bands):
    every = sorted(hops(time, band, times, bands) for time in range(times) for band in range(bands))
    wanted = KINDS * bands
    return wanted < len(every) and every[wanted - 1] < every[wanted]


def mode_columns(modes_dev):
    full = modes_dev // KINDS
    return full, modes_dev // 2 - full


def lon_tables(lon_size, bands):
    half, cosines = lon_size // 2, bands // 2
    modes_dev = lon_size // bands
    full, rest = mode_columns(modes_dev)
    points = lon_size // 4 + 1
    padded = round_up(points, LANES)
    tables = np.zeros((4, cosines * (WIDTH + QUARTER), padded), np.float64)

    def fill(kind, column, mode):
        frequency = mode - half if mode > half else mode
        radians = (frequency * np.arange(points) % lon_size) * (2.0 * math.pi / lon_size)
        wave = np.sin(radians) if mode > half else np.cos(radians)
        wave = wave * math.sqrt((1.0 if mode in (0, half) else 2.0) / lon_size)
        wave[-1] *= 0.5
        tables[kind, column, :points] = wave

    for band in range(bands):
        for parity in range(2):
            kind = 2 * (band // cosines) + parity
            for index in range(full + rest):
                mode = band * modes_dev + 2 * index + parity
                local = band % cosines
                if index < full:
                    column = local * WIDTH + index
                else:
                    column = cosines * WIDTH + local * QUARTER + index - full
                if mode == half:
                    fill(0, WIDTH - 1, mode)
                else:
                    fill(kind, column, mode)
    tables = tables.astype(np.float32)
    high = tables.astype(jnp.bfloat16)
    low = (tables - high.astype(np.float32)).astype(jnp.bfloat16)
    return np.stack([high, low], axis=1)


def lat_tables(lat_size, bands):
    lat_dev = lat_size // bands
    wavenumber = np.arange(lat_size)[:, None]
    latitude = np.arange(lat_size)[None, :]
    radians = (wavenumber * (2 * latitude + 1) % (4 * lat_size)) * (math.pi / (2.0 * lat_size))
    table = np.cos(radians) * np.where(wavenumber == 0, math.sqrt(1.0 / lat_size), math.sqrt(2.0 / lat_size))
    full = np.zeros((lat_size, bands, ROWS), np.float32)
    full[:, :, :lat_dev] = table.reshape(lat_size, bands, lat_dev)
    full = full.reshape(lat_size, bands * ROWS)

    def stacked(array):
        high = array.astype(jnp.bfloat16)
        return np.concatenate([high, (array - high.astype(np.float32)).astype(jnp.bfloat16)], axis=0)

    return stacked(full), stacked(np.ascontiguousarray(full.T))


def split(value):
    high = value.astype(jnp.bfloat16)
    low = (value - high.astype(jnp.float32)).astype(jnp.bfloat16)
    return high, low


def paired_dot(table, value):
    both = jnp.concatenate(split(value), axis=1)
    product = lax.dot_general(table, both, NN, preferred_element_type=jnp.float32)
    rows = table.shape[0] // 2
    return product[:rows, :LANES] + (product[:rows, LANES:] + product[rows:, :LANES])


def swap_halves(first, second):
    left = lax.broadcasted_iota(jnp.int32, first.shape, 1) < LANES // 2
    return (
        jnp.where(left, first, pltpu.roll(second, LANES // 2, 1)),
        jnp.where(left, pltpu.roll(first, LANES // 2, 1), second),
    )


def symmetric_gains(noise_ref, variance, scale, transition_ref, gain_ref, smoother_ref):
    hours = gain_ref.shape[0]
    transition, stationary, process = model_terms(variance, scale)
    pairs = [(0, 0), (0, 1), (0, 2), (1, 1), (1, 2), (2, 2)]
    for row in range(3):
        for column in range(3):
            transition_ref[row, column] = transition[row][column]

    def unpack(packed):
        matrix = [[None] * 3 for _ in range(3)]
        for (row, column), value in zip(pairs, packed):
            matrix[row][column] = matrix[column][row] = value
        return matrix

    def update(predicted, hour):
        inverse_var = 1.0 / (predicted[0][0] + noise_ref[hour])
        gain = [predicted[row][0] * inverse_var for row in range(3)]
        for row in range(3):
            gain_ref[hour, row] = gain[row]
        return [predicted[row][column] - gain[row] * predicted[0][column] for row, column in pairs]

    def step(hour, packed):
        covariance = unpack(packed)
        moved = mat_mul(transition, covariance)
        predicted = unpack(
            [
                moved[row][0] * transition[column][0]
                + moved[row][1] * transition[column][1]
                + moved[row][2] * transition[column][2]
                + process[row][column]
                for row, column in pairs
            ]
        )
        c00 = predicted[1][1] * predicted[2][2] - predicted[1][2] * predicted[1][2]
        c01 = predicted[0][2] * predicted[1][2] - predicted[0][1] * predicted[2][2]
        c02 = predicted[0][1] * predicted[1][2] - predicted[0][2] * predicted[1][1]
        c11 = predicted[0][0] * predicted[2][2] - predicted[0][2] * predicted[0][2]
        c12 = predicted[0][1] * predicted[0][2] - predicted[0][0] * predicted[1][2]
        c22 = predicted[0][0] * predicted[1][1] - predicted[0][1] * predicted[0][1]
        inverse_det = 1.0 / (predicted[0][0] * c00 + predicted[0][1] * c01 + predicted[0][2] * c02)
        cofactors = unpack([c00, c01, c02, c11, c12, c22])
        for row in range(3):
            scaled = [moved[within][row] * inverse_det for within in range(3)]
            for column in range(3):
                smoother_ref[hour - 1, row, column] = (
                    scaled[0] * cofactors[0][column]
                    + scaled[1] * cofactors[1][column]
                    + scaled[2] * cofactors[2][column]
                )
        return tuple(update(predicted, hour))

    first = tuple(update(stationary, 0))
    lax.fori_loop(1, hours, step, first)


def smoother_kernel(
    times,
    bands,
    observed_hbm,
    noise_hbm,
    variance_hbm,
    scale_hbm,
    forward_lat_hbm,
    inverse_lat_hbm,
    table_hbm,
    out_ref,
    observed_ref,
    noise_ref,
    block_ref,
    forward_lat_ref,
    inverse_lat_ref,
    table,
    folded,
    outbox,
    inbox,
    outbox_back,
    inbox_back,
    params_out,
    params,
    transition_ref,
    gain_ref,
    smoother_ref,
    input_sem,
    table_sem,
    send_sem,
    recv_sem,
    send_back_sem,
    recv_back_sem,
    params_send_sem,
    params_recv_sem,
):
    devices = times * bands
    cosines = bands // 2
    jobs, owners, sources = plan(times, bands)
    codes = [time * bands + band for time, band in owners]
    my_time = lax.axis_index("tm")
    my_band = lax.axis_index("space")
    me = my_time * bands + my_band
    lat_dev, lon_size = observed_ref.shape[0], observed_ref.shape[2]
    half = lon_size // 2
    hours = gain_ref.shape[0]
    n_half = gain_ref.shape[2]
    modes_dev = block_ref.shape[2]
    full, rest = mode_columns(modes_dev)
    points = table.shape[3]
    mirror = half % LANES

    def mine(places, values):
        total = 0
        for place, value in zip(places, values):
            total = total + jnp.where(me == place, value, 0)
        return total

    deep = math.isqrt(bands // 2)
    limit = max(hops(*owner, times, bands) for owner in owners)
    row, core = my_time // 2, my_time % 2
    plane, column = my_band // deep, my_band % deep

    def flip(bit, turn):
        return 1 - bit if turn else bit

    rows = [flip(row, turn) for turn in range(2)]
    near, peers = [], []
    for turn in range(bands):
        level = 2 * flip(plane // 2, turn // 4) + flip(plane % 2, turn // 2 % 2)
        across = flip(column, turn % 2)
        near.append(level + across)
        peers.append(level * deep + across)
    owning = row + near[0] <= limit

    def table_copy(kind):
        return pltpu.make_async_copy(table_hbm.at[kind], table.at[kind], table_sem.at[kind])

    inputs = [
        pltpu.make_async_copy(source, target, input_sem.at[index])
        for index, (source, target) in enumerate(
            [
                (observed_hbm, observed_ref),
                (noise_hbm, noise_ref),
                (forward_lat_hbm, forward_lat_ref),
                (inverse_lat_hbm, inverse_lat_ref),
            ]
        )
    ]
    inputs[0].start()
    table_copy(0).start()
    table_copy(1).start()
    pltpu.make_async_copy(variance_hbm, block_ref.at[0], input_sem.at[4]).start()
    pltpu.make_async_copy(scale_hbm, block_ref.at[1], input_sem.at[4]).start()
    table_copy(2).start()
    table_copy(3).start()
    for copy in inputs[1:]:
        copy.start()
    inbox[...] = jnp.zeros_like(inbox)
    inbox_back[...] = jnp.zeros_like(inbox_back)

    barrier = pltpu.get_barrier_semaphore()

    @pl.when(owning)
    def _():
        for turn in range(devices - 1, 0, -1):
            time = 2 * rows[turn // bands // 2] + flip(core, turn // bands % 2)
            pl.semaphore_signal(
                barrier, inc=1, device_id=(time, peers[turn % bands]), device_id_type=MESH
            )

    my_job = mine(codes, range(1, len(jobs) + 1)) - 1
    moved = [index for index, source in enumerate(sources) if source is not None]
    source_codes = [sources[index][0] * bands + sources[index][1] for index in moved]
    lending = mine(source_codes, [1] * len(moved)) > 0
    borrowing = mine([codes[index] for index in moved], [1] * len(moved)) > 0

    def own_modes(ref, kind):
        mode = lax.broadcasted_iota(jnp.int32, (modes_dev, LANES), 0)
        slot = lax.rem(lax.broadcasted_iota(jnp.int32, (modes_dev, LANES), 1), WIDTH)
        second = (slot >= QUARTER).astype(jnp.int32)
        place = slot - second * QUARTER
        whole = jnp.where(slot < full, 2 * slot + kind, modes_dev)
        mixed = jnp.where(place < rest, 2 * (full + place) + second, modes_dev)
        wanted = jnp.where(kind == KINDS - 1, mixed, whole)
        picked = (mode == wanted).astype(jnp.float32)
        lane = lax.broadcasted_iota(jnp.int32, (n_half, LANES), 1)
        used = wanted[:n_half] < modes_dev
        value = lax.dot_general(ref, picked, NN, precision=HIGHEST, preferred_element_type=jnp.float32)
        value = jnp.where(lane < WIDTH, value[:n_half], value[n_half:])
        return jnp.where(used, value, 1.0)

    folded[...] = jnp.zeros_like(folded)
    inputs[0].wait()
    lane = lax.broadcasted_iota(jnp.int32, (ROWS, LANES), 1)
    reverse = lax.rem(mirror + LANES - lane, LANES)
    straight = lane <= mirror

    def flipped(value):
        return jnp.take_along_axis(value, reverse, axis=1, mode="promise_in_bounds")

    def tile(value, index):
        return value[:, index * LANES : (index + 1) * LANES]

    last = half // LANES
    classes = [[], [], [], []]
    for hour in range(2):
        early = observed_ref[:, hour, :half]
        late = observed_ref[:, hour, half:]
        folded[0, hour, :lat_dev, :half] = early + late
        folded[1, hour, :lat_dev, :half] = early - late
        for parity in range(2):
            ahead = folded[parity, hour]
            turned = {index: flipped(tile(ahead, index)) for index in range(last - points // LANES, last + 1)}
            behind = jnp.concatenate(
                [
                    jnp.where(straight, turned[last - index], turned[last - index - 1])
                    for index in range(points // LANES)
                ],
                axis=1,
            )
            ahead = ahead[:, :points]
            classes[parity].append(ahead + behind if parity == 0 else ahead - behind)
            classes[2 + parity].append(ahead - behind if parity == 0 else ahead + behind)

    wide_lanes = cosines * WIDTH

    def forward(kind):
        table_copy(kind).wait()
        upper, lower = split(jnp.concatenate(classes[kind], axis=0))
        both = jnp.concatenate([upper, lower], axis=0)
        wide = lax.dot_general(both, table[kind, 0], NT, preferred_element_type=jnp.float32)
        fine = lax.dot_general(upper, table[kind, 1], NT, preferred_element_type=jnp.float32)
        return wide[: 2 * ROWS] + wide[2 * ROWS :] + fine

    def spin(value, amount):
        amount = amount % LANES
        return pltpu.roll(value, amount, 1) if amount else value

    quarter = lane // QUARTER
    middle = None

    def transform(side):
        nonlocal middle
        found = [forward(2 * side), forward(2 * side + 1)]
        base = side * KINDS * cosines
        for parity in range(2):
            for pair in range(cosines // 2):
                block = tile(found[parity], pair)
                first, second = swap_halves(block[:ROWS], block[ROWS:])
                if side == 0 and parity == 0 and pair == 0:
                    middle = spin(first, 1)
                    first = jnp.where(lax.rem(lane, WIDTH) == WIDTH - 1, 0.0, first)
                if side == 1 and parity == 0 and pair == 0:
                    first = jnp.where(lax.rem(lane, WIDTH) == 0, pltpu.roll(middle, WIDTH, 1), first)
                outbox[codes[base + parity * cosines + 2 * pair]] = first
                outbox[codes[base + parity * cosines + 2 * pair + 1]] = second
        mixed = [value[:, wide_lanes:] for value in found]
        for local in range(cosines):
            parts = [
                spin(mixed[part % 2][(part // 2) * ROWS : (part // 2 + 1) * ROWS], (part - local) * QUARTER)
                for part in range(4)
            ]
            merged = jnp.where(quarter == 0, parts[0], parts[1])
            merged = jnp.where(quarter == 2, parts[2], merged)
            outbox[codes[base + 2 * cosines + local]] = jnp.where(quarter == 3, parts[3], merged)

    def params_copy():
        target = mine(source_codes, [codes[index] for index in moved])
        return pltpu.make_async_remote_copy(
            src_ref=params_out,
            dst_ref=params,
            send_sem=params_send_sem.at[0],
            recv_sem=params_recv_sem.at[0],
            device_id=(target // bands, lax.rem(target, bands)),
            device_id_type=MESH,
        )

    def exchange(box, landing, sends, recv, slot, peer, target):
        return pltpu.make_async_remote_copy(
            src_ref=box.at[slot, pl.ds(0, lat_dev)],
            dst_ref=landing.at[target, pl.ds(0, lat_dev)],
            send_sem=sends.at[0],
            recv_sem=recv,
            device_id=peer,
            device_id_type=MESH,
        )

    def keep(box, landing, recv, slot, target):
        return pltpu.make_async_copy(
            box.at[slot, pl.ds(0, lat_dev)], landing.at[target, pl.ds(0, lat_dev)], recv
        )

    def landed(landing, recv, first, count):
        come = landing.at[pl.ds(first, count), pl.ds(0, lat_dev)]
        pltpu.make_async_copy(come, come, recv).wait()

    def send(side):
        for turn in range(1, -1, -1):
            time = 2 * rows[turn] + side
            for other in range(bands - 1, -1, -1):
                wanted = rows[turn] + near[other] <= limit
                if turn == 0 and other == 0:
                    wanted = wanted & (core != side)

                @pl.when(wanted)
                def _():
                    exchange(
                        outbox,
                        inbox,
                        send_sem,
                        recv_sem.at[my_time],
                        time * bands + peers[other],
                        (time, peers[other]),
                        me,
                    ).start()

    transform(0)
    pl.semaphore_wait(barrier, len(jobs) - owning.astype(jnp.int32))
    send(0)
    pltpu.make_async_copy(block_ref, block_ref, input_sem.at[4]).wait()

    @pl.when(lending)
    def _():
        kind = mine(source_codes, [jobs[index][1] for index in moved])
        params_out[0] = own_modes(block_ref[0], kind)
        params_out[1] = own_modes(block_ref[1], kind)
        params_copy().start()

    transform(1)
    send(1)

    for copy in inputs[1:]:
        copy.wait()

    @pl.when(owning)
    def _():
        keep(outbox, inbox, recv_sem.at[my_time], me, me).start()

        @pl.when(jnp.logical_not(borrowing))
        def _():
            kind = mine(codes, [kind for _, kind in jobs])
            params[0] = own_modes(block_ref[0], kind)
            params[1] = own_modes(block_ref[1], kind)

        @pl.when(borrowing)
        def _():
            pltpu.make_async_copy(params, params, params_recv_sem.at[0]).wait()

        symmetric_gains(noise_ref, params[0], params[1], transition_ref, gain_ref, smoother_ref)

        spectra = []
        for time in range(times):
            landed(inbox, recv_sem.at[time], time * bands, bands)
            arrived = inbox[time * bands : (time + 1) * bands].reshape(bands * ROWS, LANES)
            mixed = paired_dot(forward_lat_ref[...], arrived)
            spectra.extend(swap_halves(mixed[:n_half], mixed[n_half:]))

        transition = [[transition_ref[row, column] for column in range(3)] for row in range(3)]
        means, predictions = [], [None]
        means.append([gain_ref[0, row] * spectra[0] for row in range(3)])
        for hour in range(1, hours):
            predicted = mat_vec(transition, means[-1])
            residual = spectra[hour] - predicted[0]
            predictions.append(predicted)
            means.append([predicted[row] + gain_ref[hour, row] * residual for row in range(3)])
        smoothed = means[-1]
        series = [None] * hours
        series[hours - 1] = smoothed[0]
        for hour in range(hours - 2, -1, -1):
            difference = [smoothed[row] - predictions[hour + 1][row] for row in range(3)]
            smoothed = [
                means[hour][row]
                + smoother_ref[hour, row, 0] * difference[0]
                + smoother_ref[hour, row, 1] * difference[1]
                + smoother_ref[hour, row, 2] * difference[2]
                for row in range(3)
            ]
            series[hour] = smoothed[0]

        for time in range(times):
            stacked = jnp.concatenate(swap_halves(series[2 * time], series[2 * time + 1]), axis=0)
            grid = paired_dot(inverse_lat_ref[...], stacked)
            outbox_back[time * bands : (time + 1) * bands] = grid.reshape(bands, ROWS, LANES)
            for other in range(bands - 1, -1, -1):
                copy = exchange(
                    outbox_back,
                    inbox_back,
                    send_back_sem,
                    recv_back_sem.at[core],
                    time * bands + peers[other],
                    (time, peers[other]),
                    my_job,
                )
                if other == 0:
                    pl.when(my_time != time)(copy.start)
                else:
                    copy.start()

        keep(outbox_back, inbox_back, recv_back_sem.at[core], me, my_job).start()

    grids = []
    for side in range(2):
        base = side * KINDS * cosines
        landed(inbox_back, recv_back_sem.at[side], base, KINDS * cosines)
        boxes = [
            [inbox_back[base + kind * cosines + local] for local in range(cosines)] for kind in range(KINDS)
        ]
        for parity in range(2):
            blocks = []
            for pair in range(cosines // 2):
                blocks.append(list(swap_halves(*boxes[parity][2 * pair : 2 * pair + 2])))
            shared = []
            for hour in range(2):
                merged = None
                for local in range(cosines):
                    part = spin(boxes[2][local], (local - (2 * hour + parity)) * QUARTER)
                    merged = part if merged is None else jnp.where(quarter == local, part, merged)
                shared.append(merged)
            blocks.append(shared)
            upper, lower = split(
                jnp.concatenate([jnp.concatenate(block, axis=0) for block in blocks], axis=1)
            )
            both = jnp.concatenate([upper, lower], axis=0)
            kind = 2 * side + parity
            wide = lax.dot_general(both, table[kind, 0], NN, preferred_element_type=jnp.float32)
            fine = lax.dot_general(upper, table[kind, 1], NN, preferred_element_type=jnp.float32)
            grids.append(wide[: 2 * ROWS] + wide[2 * ROWS :] + fine)

    origin = inbox_back[KINDS * cosines]
    alternating = jnp.where(lax.rem(lane, 2) == 0, 1.0, -1.0) * math.sqrt(1.0 / lon_size)
    lifted = []
    for hour in range(2):
        value = jnp.broadcast_to(origin[:, hour * WIDTH : hour * WIDTH + 1], (ROWS, LANES)) * alternating
        edge = jnp.where(lane == half // 2 % LANES, 0.5 * value, value)
        lifted.append(jnp.concatenate([value] * (points // LANES - 1) + [edge], axis=1))
    grids[0] = grids[0] + jnp.concatenate(lifted, axis=0)

    count = points // LANES
    for hour in range(2):
        even_cos, odd_cos, even_sin, odd_sin = [grid[hour * ROWS : (hour + 1) * ROWS] for grid in grids]
        ahead, ahead_odd = even_cos + even_sin, odd_cos + odd_sin
        behind, behind_odd = even_cos - even_sin, odd_sin - odd_cos
        for side in range(2):
            start = ahead + ahead_odd if side == 0 else ahead - ahead_odd
            end = behind + behind_odd if side == 0 else behind - behind_odd
            turned = [flipped(tile(end, index)) for index in range(count)]
            pieces = [tile(start, index) for index in range(count - 1)]
            border = half // 2 - (count - 1) * LANES
            fold = tile(start, count - 1)
            fold = jnp.where(lane == border, fold + fold, fold)
            pieces.append(jnp.where(lane <= border, fold, turned[count - 1]))
            for index in range(count - 1, 0, -1):
                pieces.append(jnp.where(straight, turned[index], turned[index - 1]))
            pieces.append(turned[0])
            row = jnp.concatenate(pieces, axis=1)
            out_ref[:, hour, side * half : (side + 1) * half] = row[:lat_dev, :half]

    def gone(box, sends, count):
        left = box.at[pl.ds(0, count), pl.ds(0, lat_dev)]
        pltpu.make_async_copy(left, left, sends.at[0]).wait()

    gone(outbox, send_sem, len(jobs) - 1)

    @pl.when(jnp.logical_not(owning))
    def _():
        gone(outbox, send_sem, 1)

    @pl.when(owning)
    def _():
        gone(outbox_back, send_back_sem, devices - 1)

    @pl.when(lending)
    def _():
        pltpu.make_async_copy(params_out, params_out, params_send_sem.at[0]).wait()


def per_device_fused(observed, noise_var, spectral_var, time_scale):
    times, bands = lax.axis_size("tm"), lax.axis_size("space")
    hours_dev, lat_dev, lon_size = observed.shape
    hours, lat_size = noise_var.shape[0], spectral_var.shape[1]
    n_half = lat_size // 2
    half_padded = round_up(lon_size // 2, LANES)
    n_jobs = KINDS * bands

    table = lon_tables(lon_size, bands)
    forward_lat, inverse_lat = lat_tables(lat_size, bands)
    in_vmem = pl.BlockSpec(memory_space=pltpu.VMEM)
    in_place = pl.BlockSpec(memory_space=pltpu.HBM)
    box = pltpu.VMEM((times * bands, ROWS, LANES), jnp.float32)
    job_box = pltpu.VMEM((n_jobs, ROWS, LANES), jnp.float32)
    dma = pltpu.SemaphoreType.DMA
    field = pl.pallas_call(
        functools.partial(smoother_kernel, times, bands),
        out_shape=pltpu.VMEM((lat_dev, hours_dev, lon_size), jnp.float32),
        in_specs=[in_place] * 7,
        out_specs=in_vmem,
        scratch_shapes=[
            pltpu.VMEM((lat_dev, hours_dev, lon_size), jnp.float32),
            pltpu.SMEM((hours,), jnp.float32),
            pltpu.VMEM((2, lat_size, spectral_var.shape[0]), jnp.float32),
            pltpu.VMEM(forward_lat.shape, jnp.bfloat16),
            pltpu.VMEM(inverse_lat.shape, jnp.bfloat16),
            pltpu.VMEM(table.shape, jnp.bfloat16),
            pltpu.VMEM((2, 2, ROWS, half_padded), jnp.float32),
            box,
            box,
            box,
            job_box,
            pltpu.VMEM((2, n_half, LANES), jnp.float32),
            pltpu.VMEM((2, n_half, LANES), jnp.float32),
            pltpu.VMEM((3, 3, n_half, LANES), jnp.float32),
            pltpu.VMEM((hours, 3, n_half, LANES), jnp.float32),
            pltpu.VMEM((hours, 3, 3, n_half, LANES), jnp.float32),
            dma((5,)),
            dma((4,)),
            dma((1,)),
            dma((times,)),
            dma((1,)),
            dma((2,)),
            dma((1,)),
            dma((1,)),
        ],
        compiler_params=pltpu.CompilerParams(collective_id=0, has_side_effects=True),
    )(
        observed.transpose(1, 0, 2),
        noise_var,
        spectral_var.T,
        time_scale.T,
        jnp.asarray(forward_lat),
        jnp.asarray(inverse_lat),
        jnp.asarray(table),
    )
    return field.transpose(1, 0, 2)


def fits(observed, spectral_var):
    times, bands = lax.axis_size("tm"), lax.axis_size("space")
    hours_dev, lat_dev, lon_size = observed.shape
    modes_dev, lat_size = spectral_var.shape
    full, rest = mode_columns(modes_dev)
    half, points = lon_size // 2, round_up(lon_size // 4 + 1, LANES)
    return (
        hours_dev == 2
        and lat_dev <= ROWS
        and lat_size % (2 * ROWS) == 0
        and times == KINDS + 1
        and balanced(times, bands)
        and 2 * math.isqrt(bands // 2) ** 2 == bands
        and bands == LANES // 16
        and lon_size % 4 == 0
        and modes_dev % 2 == 0
        and modes_dev % KINDS == 0
        and full < WIDTH
        and rest <= QUARTER
        and half % LANES > 0
        and round_up(half, LANES) == 2 * points
        and half // 2 >= points - LANES
    )


def per_device(observed, noise_var, spectral_var, time_scale):
    if fits(observed, spectral_var):
        return per_device_fused(observed, noise_var, spectral_var, time_scale)
    return per_device_general(observed, noise_var, spectral_var, time_scale)


def solution(mesh):
    placed = (P("tm", "space", None), P(), P("space", None), P("space", None))
    return jax.shard_map(
        per_device, mesh=mesh, in_specs=placed, out_specs=P("tm", "space", None), check_vma=False
    )
```

```python
import functools
import math

import jax
import jax.numpy as jnp
import numpy as np
from jax import lax
from jax.experimental import pallas as pl
from jax.experimental.pallas import tpu as pltpu
from jax.sharding import PartitionSpec as P

HIGHEST = lax.Precision.HIGHEST
ROOT_FIVE = 2.23606797749979
NILPOTENT = ((1.0, 1.0, 0.0), (0.0, 1.0, 1.0), (-1.0, -3.0, -2.0))
NILPOTENT_SQUARED = ((1.0, 2.0, 1.0), (-1.0, -2.0, -1.0), (1.0, 2.0, 1.0))
STATIONARY = ((1.0, 0.0, -1.0 / 3.0), (0.0, 1.0 / 3.0, 0.0), (-1.0 / 3.0, 0.0, 1.0))


def lon_basis(size):
    mode_index = lax.broadcasted_iota(jnp.int32, (size, size), 0)
    longitude = lax.broadcasted_iota(jnp.int32, (size, size), 1)
    half_size = size // 2
    sine_rows = mode_index > half_size
    frequency = jnp.where(sine_rows, mode_index - half_size, mode_index)
    radians = (frequency * longitude % size).astype(jnp.float32) * (2.0 * math.pi / size)
    waveform = jnp.where(sine_rows, jnp.sin(radians), jnp.cos(radians))
    edge_rows = (mode_index == 0) | (mode_index == half_size)
    weight = jnp.where(edge_rows, math.sqrt(1.0 / size), math.sqrt(2.0 / size))
    return waveform * weight


def lat_basis(size):
    wavenumber = lax.broadcasted_iota(jnp.int32, (size, size), 0)
    latitude = lax.broadcasted_iota(jnp.int32, (size, size), 1)
    radians = (wavenumber * (2 * latitude + 1) % (4 * size)).astype(jnp.float32) * (
        math.pi / (2.0 * size)
    )
    weight = jnp.where(wavenumber == 0, math.sqrt(1.0 / size), math.sqrt(2.0 / size))
    return jnp.cos(radians) * weight


def mat_mul(left, right):
    return [
        [
            left[across][0] * right[0][within]
            + left[across][1] * right[1][within]
            + left[across][2] * right[2][within]
            for within in range(3)
        ]
        for across in range(3)
    ]


def mat_vec(matrix, vector):
    return [
        matrix[across][0] * vector[0]
        + matrix[across][1] * vector[1]
        + matrix[across][2] * vector[2]
        for across in range(3)
    ]


def transposed(matrix):
    return [[matrix[within][across] for within in range(3)] for across in range(3)]


def inverted(matrix):
    cofactor = [
        [
            matrix[1][1] * matrix[2][2] - matrix[1][2] * matrix[2][1],
            matrix[0][2] * matrix[2][1] - matrix[0][1] * matrix[2][2],
            matrix[0][1] * matrix[1][2] - matrix[0][2] * matrix[1][1],
        ],
        [
            matrix[1][2] * matrix[2][0] - matrix[1][0] * matrix[2][2],
            matrix[0][0] * matrix[2][2] - matrix[0][2] * matrix[2][0],
            matrix[0][2] * matrix[1][0] - matrix[0][0] * matrix[1][2],
        ],
        [
            matrix[1][0] * matrix[2][1] - matrix[1][1] * matrix[2][0],
            matrix[0][1] * matrix[2][0] - matrix[0][0] * matrix[2][1],
            matrix[0][0] * matrix[1][1] - matrix[0][1] * matrix[1][0],
        ],
    ]
    determinant = (
        matrix[0][0] * cofactor[0][0]
        + matrix[0][1] * cofactor[1][0]
        + matrix[0][2] * cofactor[2][0]
    )
    return [[cofactor[across][within] / determinant for within in range(3)] for across in range(3)]


def model_terms(variance, scale):
    decay_rate = ROOT_FIVE / scale
    damping = jnp.exp(-decay_rate)
    transition = [
        [
            damping
            * (
                (1.0 if across == within else 0.0)
                + decay_rate * NILPOTENT[across][within]
                + 0.5 * decay_rate * decay_rate * NILPOTENT_SQUARED[across][within]
            )
            for within in range(3)
        ]
        for across in range(3)
    ]
    stationary = [
        [variance * STATIONARY[across][within] for within in range(3)] for across in range(3)
    ]
    carried = mat_mul(mat_mul(transition, stationary), transposed(transition))
    process_noise = [
        [stationary[across][within] - carried[across][within] for within in range(3)]
        for across in range(3)
    ]
    return (transition, stationary, process_noise)


def predict_cov(covariance, transition, process_noise):
    carried = mat_mul(mat_mul(transition, covariance), transposed(transition))
    return [
        [carried[across][within] + process_noise[across][within] for within in range(3)]
        for across in range(3)
    ]


def gain_and_cov(predicted_cov, noise):
    innovation_var = predicted_cov[0][0] + noise
    kalman_gain = [predicted_cov[across][0] / innovation_var for across in range(3)]
    covariance = [
        [
            predicted_cov[across][within] - kalman_gain[across] * predicted_cov[0][within]
            for within in range(3)
        ]
        for across in range(3)
    ]
    return (kalman_gain, covariance)


def smooth_series(spectra, noise_var, variance, scale):
    transition, stationary, process_noise = model_terms(variance, scale)
    zeros = jnp.zeros_like(variance)

    def forward(carry, inputs):
        mean_state, covariance = carry
        observed, noise = inputs
        predicted_cov = predict_cov(covariance, transition, process_noise)
        smoother_gain = mat_mul(
            mat_mul(covariance, transposed(transition)), inverted(predicted_cov)
        )
        predicted = mat_vec(transition, mean_state)
        kalman_gain, covariance = gain_and_cov(predicted_cov, noise)
        residual = observed - predicted[0]
        mean_state = [predicted[across] + kalman_gain[across] * residual for across in range(3)]
        return ((mean_state, covariance), (mean_state, smoother_gain))

    _, (means, gains) = lax.scan(forward, ([zeros, zeros, zeros], stationary), (spectra, noise_var))

    def backward(later, inputs):
        mean_state, smoother_gain = inputs
        projected = mat_vec(transition, mean_state)
        difference = [later[across] - projected[across] for across in range(3)]
        correction = mat_vec(smoother_gain, difference)
        smoothed_state = [mean_state[across] + correction[across] for across in range(3)]
        return (smoothed_state, smoothed_state[0])

    last_state = [means[across][-1] for across in range(3)]
    earlier_means = [means[across][:-1] for across in range(3)]
    next_gains = [[gains[across][within][1:] for within in range(3)] for across in range(3)]
    _, field = lax.scan(backward, last_state, (earlier_means, next_gains), reverse=True)
    return jnp.concatenate([field, last_state[0][None]], axis=0)


def per_device_general(observed, noise_var, spectral_var, time_scale):
    hours_dev, lat_dev, lon_size = observed.shape
    band_count = lax.axis_size("space")
    lat_size = lat_dev * band_count
    modes_dev = lon_size // band_count
    lon_table = lon_basis(lon_size)
    lat_table = lat_basis(lat_size).reshape(lat_size, band_count, lat_dev)
    grid_rows = observed.reshape(hours_dev * lat_dev, lon_size)
    spectra = lax.dot_general(lon_table, grid_rows, (((1,), (1,)), ((), ())), precision=HIGHEST)
    by_mode = lax.all_to_all(spectra, "space", split_axis=0, concat_axis=1, tiled=True)
    by_mode = by_mode.reshape(modes_dev, band_count, hours_dev, lat_dev)
    coefficients = jnp.einsum("msha,nsa->hmn", by_mode, lat_table, precision=HIGHEST)
    flat = coefficients.reshape(hours_dev, modes_dev * lat_size)
    hourly = lax.all_to_all(flat, "tm", split_axis=1, concat_axis=0, tiled=True)
    share = flat.shape[1] // lax.axis_size("tm")
    offset = lax.axis_index("tm") * share
    variance = lax.dynamic_slice_in_dim(spectral_var.reshape(-1), offset, share)
    scale = lax.dynamic_slice_in_dim(time_scale.reshape(-1), offset, share)
    series = smooth_series(hourly, noise_var, variance, scale)
    smooth = lax.all_to_all(series, "tm", split_axis=0, concat_axis=1, tiled=True).reshape(
        hours_dev, modes_dev, lat_size
    )
    latitude_grid = jnp.einsum("hmn,nsa->msha", smooth, lat_table, precision=HIGHEST)
    latitude_grid = latitude_grid.reshape(modes_dev, band_count * hours_dev * lat_dev)
    by_band = lax.all_to_all(latitude_grid, "space", split_axis=1, concat_axis=0, tiled=True)
    field = lax.dot_general(by_band, lon_table, (((0,), (0,)), ((), ())), precision=HIGHEST)
    return field.reshape(hours_dev, lat_dev, lon_size)


LANES = 128
ROWS = 8
MESH = pl.DeviceIdType.MESH
NT = (((1,), (1,)), ((), ()))
NN = (((1,), (0,)), ((), ()))


def round_up(value, unit):
    return -(-value // unit) * unit


KINDS = 3
WIDTH = LANES // 2
QUARTER = LANES // 4


def hops(time, band, times, bands):
    wide = math.isqrt(bands // 2)
    return time // 2 + band // wide + band % wide


def plan(times, bands):
    cosines = bands // 2
    jobs = [
        (band, kind)
        for base in (0, cosines)
        for kind in range(KINDS)
        for band in range(base, base + cosines)
    ]
    devices = [(time, band) for time in range(times) for band in range(bands)]
    chosen = sorted(devices, key=lambda d: (hops(*d, times, bands), d))[: len(jobs)]
    owner, sources, used = {}, {}, {}
    for band in range(bands):
        for kind, device in enumerate(sorted(d for d in chosen if d[1] == band)[:KINDS]):
            owner[band, kind] = device
    taken = set(owner.values())
    free = sorted((d for d in chosen if d not in taken), key=lambda d: -hops(*d, times, bands))
    for job in jobs:
        if job not in owner:
            owner[job] = free.pop(0)
            sources[job] = (used.get(job[0], 0), job[0])
            used[job[0]] = sources[job][0] + 1
    return jobs, [owner[job] for job in jobs], [sources.get(job) for job in jobs]


def balanced(times, bands):
    every = sorted(hops(time, band, times, bands) for time in range(times) for band in range(bands))
    wanted = KINDS * bands
    lower = max(hops(time, band, times, bands) for time in range(times) for band in range(bands // 2))
    return wanted < len(every) and lower <= every[wanted - 1] < every[wanted]


def mode_columns(modes_dev):
    full = modes_dev // KINDS
    return full, modes_dev // 2 - full


def lon_tables(lon_size, bands):
    half, cosines = lon_size // 2, bands // 2
    modes_dev = lon_size // bands
    full, rest = mode_columns(modes_dev)
    points = lon_size // 4 + 1
    padded = round_up(points, LANES)
    tables = np.zeros((4, cosines * (WIDTH + QUARTER), padded), np.float64)

    def fill(kind, column, mode):
        frequency = mode - half if mode > half else mode
        radians = (frequency * np.arange(points) % lon_size) * (2.0 * math.pi / lon_size)
        wave = np.sin(radians) if mode > half else np.cos(radians)
        wave = wave * math.sqrt((1.0 if mode in (0, half) else 2.0) / lon_size)
        wave[-1] *= 0.5
        tables[kind, column, :points] = wave

    for band in range(bands):
        for parity in range(2):
            kind = 2 * (band // cosines) + parity
            for index in range(full + rest):
                mode = band * modes_dev + 2 * index + parity
                local = band % cosines
                if index < full:
                    column = local * WIDTH + index
                else:
                    column = cosines * WIDTH + local * QUARTER + index - full
                if mode == half:
                    fill(0, WIDTH - 1, mode)
                else:
                    fill(kind, column, mode)
    tables = tables.astype(np.float32)
    high = tables.astype(jnp.bfloat16)
    low = (tables - high.astype(np.float32)).astype(jnp.bfloat16)
    return np.stack([high, low], axis=1)


def lat_tables(lat_size, bands):
    lat_dev = lat_size // bands
    wavenumber = np.arange(lat_size)[:, None]
    latitude = np.arange(lat_size)[None, :]
    radians = (wavenumber * (2 * latitude + 1) % (4 * lat_size)) * (math.pi / (2.0 * lat_size))
    table = np.cos(radians) * np.where(wavenumber == 0, math.sqrt(1.0 / lat_size), math.sqrt(2.0 / lat_size))
    full = np.zeros((lat_size, bands, ROWS), np.float32)
    full[:, :, :lat_dev] = table.reshape(lat_size, bands, lat_dev)
    full = full.reshape(lat_size, bands * ROWS)

    def stacked(array):
        high = array.astype(jnp.bfloat16)
        return np.concatenate([high, (array - high.astype(np.float32)).astype(jnp.bfloat16)], axis=0)

    return stacked(full), stacked(np.ascontiguousarray(full.T))


def split(value):
    high = value.astype(jnp.bfloat16)
    low = (value - high.astype(jnp.float32)).astype(jnp.bfloat16)
    return high, low


def paired_dot(table, value):
    both = jnp.concatenate(split(value), axis=1)
    product = lax.dot_general(table, both, NN, preferred_element_type=jnp.float32)
    rows = table.shape[0] // 2
    return product[:rows, :LANES] + (product[:rows, LANES:] + product[rows:, :LANES])


def swap_halves(first, second):
    left = lax.broadcasted_iota(jnp.int32, first.shape, 1) < LANES // 2
    return (
        jnp.where(left, first, pltpu.roll(second, LANES // 2, 1)),
        jnp.where(left, pltpu.roll(first, LANES // 2, 1), second),
    )


def symmetric_gains(noise_ref, variance, scale, transition_ref, gain_ref, smoother_ref):
    hours = gain_ref.shape[0]
    transition, stationary, process = model_terms(variance, scale)
    pairs = [(0, 0), (0, 1), (0, 2), (1, 1), (1, 2), (2, 2)]
    for row in range(3):
        for column in range(3):
            transition_ref[row, column] = transition[row][column]

    def unpack(packed):
        matrix = [[None] * 3 for _ in range(3)]
        for (row, column), value in zip(pairs, packed):
            matrix[row][column] = matrix[column][row] = value
        return matrix

    def update(predicted, hour):
        inverse_var = 1.0 / (predicted[0][0] + noise_ref[hour])
        gain = [predicted[row][0] * inverse_var for row in range(3)]
        for row in range(3):
            gain_ref[hour, row] = gain[row]
        return [predicted[row][column] - gain[row] * predicted[0][column] for row, column in pairs]

    def step(hour, packed):
        covariance = unpack(packed)
        moved = mat_mul(transition, covariance)
        predicted = unpack(
            [
                moved[row][0] * transition[column][0]
                + moved[row][1] * transition[column][1]
                + moved[row][2] * transition[column][2]
                + process[row][column]
                for row, column in pairs
            ]
        )
        c00 = predicted[1][1] * predicted[2][2] - predicted[1][2] * predicted[1][2]
        c01 = predicted[0][2] * predicted[1][2] - predicted[0][1] * predicted[2][2]
        c02 = predicted[0][1] * predicted[1][2] - predicted[0][2] * predicted[1][1]
        c11 = predicted[0][0] * predicted[2][2] - predicted[0][2] * predicted[0][2]
        c12 = predicted[0][1] * predicted[0][2] - predicted[0][0] * predicted[1][2]
        c22 = predicted[0][0] * predicted[1][1] - predicted[0][1] * predicted[0][1]
        inverse_det = 1.0 / (predicted[0][0] * c00 + predicted[0][1] * c01 + predicted[0][2] * c02)
        cofactors = unpack([c00, c01, c02, c11, c12, c22])
        for row in range(3):
            scaled = [moved[within][row] * inverse_det for within in range(3)]
            for column in range(3):
                smoother_ref[hour - 1, row, column] = (
                    scaled[0] * cofactors[0][column]
                    + scaled[1] * cofactors[1][column]
                    + scaled[2] * cofactors[2][column]
                )
        return tuple(update(predicted, hour))

    first = tuple(update(stationary, 0))
    lax.fori_loop(1, hours, step, first)


def smoother_kernel(
    times,
    bands,
    observed_hbm,
    noise_hbm,
    variance_hbm,
    scale_hbm,
    forward_lat_hbm,
    inverse_lat_hbm,
    table_hbm,
    out_ref,
    observed_ref,
    noise_ref,
    block_ref,
    forward_lat_ref,
    inverse_lat_ref,
    table,
    folded,
    outbox_cos,
    outbox_sin,
    inbox,
    back_0,
    back_1,
    back_2,
    back_3,
    inbox_back,
    params_out,
    params,
    transition_ref,
    gain_ref,
    smoother_ref,
    input_sem,
    table_sem,
    send_sem,
    recv_sem,
    send_back_sem,
    recv_back_sem,
    params_send_sem,
    params_recv_sem,
):
    devices = times * bands
    cosines = bands // 2
    outboxes = (outbox_cos, outbox_sin)
    boxes_back = (back_0, back_1, back_2, back_3)
    jobs, owners, sources = plan(times, bands)
    codes = [time * bands + band for time, band in owners]
    my_time = lax.axis_index("tm")
    my_band = lax.axis_index("space")
    me = my_time * bands + my_band
    lat_dev, lon_size = observed_ref.shape[0], observed_ref.shape[2]
    half = lon_size // 2
    hours = gain_ref.shape[0]
    n_half = gain_ref.shape[2]
    modes_dev = block_ref.shape[2]
    full, rest = mode_columns(modes_dev)
    points = table.shape[3]
    mirror = half % LANES

    def mine(places, values):
        total = 0
        for place, value in zip(places, values):
            total = total + jnp.where(me == place, value, 0)
        return total

    deep = math.isqrt(bands // 2)
    limit = max(hops(*owner, times, bands) for owner in owners)
    row, core = my_time // 2, my_time % 2
    plane, column = my_band // deep, my_band % deep

    def flip(bit, turn):
        return 1 - bit if turn else bit

    rows = [flip(row, turn) for turn in range(2)]
    near, peers = [], []
    for turn in range(bands):
        level = 2 * flip(plane // 2, turn // 4) + flip(plane % 2, turn // 2 % 2)
        across = flip(column, turn % 2)
        near.append(level + across)
        peers.append(level * deep + across)
    owning = row + near[0] <= limit

    def table_copy(kind):
        return pltpu.make_async_copy(table_hbm.at[kind], table.at[kind], table_sem.at[kind])

    inputs = [
        pltpu.make_async_copy(source, target, input_sem.at[index])
        for index, (source, target) in enumerate(
            [
                (observed_hbm, observed_ref),
                (noise_hbm, noise_ref),
                (forward_lat_hbm, forward_lat_ref),
                (inverse_lat_hbm, inverse_lat_ref),
            ]
        )
    ]
    pltpu.make_async_copy(variance_hbm, block_ref.at[0], input_sem.at[4]).start()
    pltpu.make_async_copy(scale_hbm, block_ref.at[1], input_sem.at[4]).start()
    inputs[0].start()
    table_copy(0).start()
    table_copy(1).start()
    table_copy(2).start()
    table_copy(3).start()
    for copy in inputs[1:]:
        copy.start()
    inbox[...] = jnp.zeros_like(inbox)
    inbox_back[...] = jnp.zeros_like(inbox_back)

    barrier = pltpu.get_barrier_semaphore()

    @pl.when(owning)
    def _():
        for turn in range(devices - 1, 0, -1):
            time = 2 * rows[turn // bands // 2] + flip(core, turn // bands % 2)
            pl.semaphore_signal(
                barrier, inc=1, device_id=(time, peers[turn % bands]), device_id_type=MESH
            )

    my_job = mine(codes, range(1, len(jobs) + 1)) - 1
    moved = [index for index, source in enumerate(sources) if source is not None]
    source_codes = [sources[index][0] * bands + sources[index][1] for index in moved]
    lending = mine(source_codes, [1] * len(moved)) > 0
    borrowing = mine([codes[index] for index in moved], [1] * len(moved)) > 0

    def own_modes(ref, kind):
        mode = lax.broadcasted_iota(jnp.int32, (modes_dev, LANES), 0)
        slot = lax.rem(lax.broadcasted_iota(jnp.int32, (modes_dev, LANES), 1), WIDTH)
        second = (slot >= QUARTER).astype(jnp.int32)
        place = slot - second * QUARTER
        whole = jnp.where(slot < full, 2 * slot + kind, modes_dev)
        mixed = jnp.where(place < rest, 2 * (full + place) + second, modes_dev)
        wanted = jnp.where(kind == KINDS - 1, mixed, whole)
        picked = (mode == wanted).astype(jnp.float32)
        lane = lax.broadcasted_iota(jnp.int32, (n_half, LANES), 1)
        used = wanted[:n_half] < modes_dev
        value = lax.dot_general(ref, picked, NN, precision=HIGHEST, preferred_element_type=jnp.float32)
        value = jnp.where(lane < WIDTH, value[:n_half], value[n_half:])
        return jnp.where(used, value, 1.0)

    folded[...] = jnp.zeros_like(folded)
    pltpu.make_async_copy(block_ref, block_ref, input_sem.at[4]).wait()

    @pl.when(lending)
    def _():
        kind = mine(source_codes, [jobs[index][1] for index in moved])
        params_out[0] = own_modes(block_ref[0], kind)
        params_out[1] = own_modes(block_ref[1], kind)

    inputs[0].wait()
    lane = lax.broadcasted_iota(jnp.int32, (ROWS, LANES), 1)
    reverse = lax.rem(mirror + LANES - lane, LANES)
    straight = lane <= mirror

    def flipped(value):
        return jnp.take_along_axis(value, reverse, axis=1, mode="promise_in_bounds")

    def tile(value, index):
        return value[:, index * LANES : (index + 1) * LANES]

    last = half // LANES
    classes = [[], [], [], []]
    for hour in range(2):
        early = observed_ref[:, hour, :half]
        late = observed_ref[:, hour, half:]
        folded[0, hour, :lat_dev, :half] = early + late
        folded[1, hour, :lat_dev, :half] = early - late
        for parity in range(2):
            ahead = folded[parity, hour]
            turned = {index: flipped(tile(ahead, index)) for index in range(last - points // LANES, last + 1)}
            behind = jnp.concatenate(
                [
                    jnp.where(straight, turned[last - index], turned[last - index - 1])
                    for index in range(points // LANES)
                ],
                axis=1,
            )
            ahead = ahead[:, :points]
            classes[parity].append(ahead + behind if parity == 0 else ahead - behind)
            classes[2 + parity].append(ahead - behind if parity == 0 else ahead + behind)

    wide_lanes = cosines * WIDTH

    def forward(kind):
        table_copy(kind).wait()
        upper, lower = split(jnp.concatenate(classes[kind], axis=0))
        both = jnp.concatenate([upper, lower], axis=0)
        wide = lax.dot_general(both, table[kind, 0], NT, preferred_element_type=jnp.float32)
        fine = lax.dot_general(upper, table[kind, 1], NT, preferred_element_type=jnp.float32)
        return wide[: 2 * ROWS] + wide[2 * ROWS :] + fine

    def spin(value, amount):
        amount = amount % LANES
        return pltpu.roll(value, amount, 1) if amount else value

    quarter = lane // QUARTER
    middle = None

    def transform(side):
        nonlocal middle
        found = [forward(2 * side), forward(2 * side + 1)]
        base = side * KINDS * cosines
        for parity in range(2):
            for pair in range(cosines // 2):
                block = tile(found[parity], pair)
                first, second = swap_halves(block[:ROWS], block[ROWS:])
                if side == 0 and parity == 0 and pair == 0:
                    middle = spin(first, 1)
                    first = jnp.where(lax.rem(lane, WIDTH) == WIDTH - 1, 0.0, first)
                if side == 1 and parity == 0 and pair == 0:
                    first = jnp.where(lax.rem(lane, WIDTH) == 0, pltpu.roll(middle, WIDTH, 1), first)
                outboxes[side][codes[base + parity * cosines + 2 * pair]] = first
                outboxes[side][codes[base + parity * cosines + 2 * pair + 1]] = second
        mixed = [value[:, wide_lanes:] for value in found]
        for local in range(cosines):
            parts = [
                spin(mixed[part % 2][(part // 2) * ROWS : (part // 2 + 1) * ROWS], (part - local) * QUARTER)
                for part in range(4)
            ]
            merged = jnp.where(quarter == 0, parts[0], parts[1])
            merged = jnp.where(quarter == 2, parts[2], merged)
            outboxes[side][codes[base + 2 * cosines + local]] = jnp.where(quarter == 3, parts[3], merged)

    def params_copy():
        target = mine(source_codes, [codes[index] for index in moved])
        return pltpu.make_async_remote_copy(
            src_ref=params_out,
            dst_ref=params,
            send_sem=params_send_sem.at[0],
            recv_sem=params_recv_sem.at[0],
            device_id=(target // bands, lax.rem(target, bands)),
            device_id_type=MESH,
        )

    def exchange(box, landing, sends, recv, slot, peer, target):
        return pltpu.make_async_remote_copy(
            src_ref=box.at[slot, pl.ds(0, lat_dev)],
            dst_ref=landing.at[target, pl.ds(0, lat_dev)],
            send_sem=sends.at[0],
            recv_sem=recv,
            device_id=peer,
            device_id_type=MESH,
        )

    def keep(box, landing, recv, slot, target):
        return pltpu.make_async_copy(
            box.at[slot, pl.ds(0, lat_dev)], landing.at[target, pl.ds(0, lat_dev)], recv
        )

    def landed(landing, recv, first, count):
        come = landing.at[pl.ds(first, count), pl.ds(0, lat_dev)]
        pltpu.make_async_copy(come, come, recv).wait()

    def forth(box, time, band, wanted):
        @pl.when(wanted)
        def _():
            exchange(
                box, inbox, send_sem, recv_sem.at[my_time], time * bands + band, (time, band), me
            ).start()

    upper_half = plane // 2

    def place(top, turn):
        level = 2 * top + flip(plane % 2, turn // 2)
        across = flip(column, turn % 2)
        return level * deep + across, level + across

    def send(side):
        for turn in range(times - 1, -1, -1):
            next_row, next_core = rows[turn // 2], flip(core, turn % 2)
            for other in range(deep * deep - 1, -1, -1):
                band, height = place(side, other)
                if side == 0:
                    wanted = next_row + next_core < 2
                else:
                    wanted = next_row + height <= limit
                if turn == 0 and other == 0:
                    wanted = wanted & (upper_half != side)
                forth(outboxes[side], 2 * next_row + next_core, band, wanted)
        if side == 1:
            for other in range(deep * deep - 1, -1, -1):
                band, _ = place(0, other)
                wanted = (my_time != times - 1) | (upper_half != 0) if other == 0 else my_time >= 0
                forth(outboxes[1], times - 1, band, wanted)

    transform(0)
    pl.semaphore_wait(barrier, len(jobs) - owning.astype(jnp.int32))

    @pl.when(lending)
    def _():
        params_copy().start()

    send(0)
    transform(1)
    send(1)

    for copy in inputs[1:]:
        copy.wait()

    @pl.when(owning)
    def _():
        for side in range(2):
            inside = (my_job < KINDS * cosines) == (side == 0)
            pl.when(inside)(keep(outboxes[side], inbox, recv_sem.at[my_time], me, me).start)

        @pl.when(jnp.logical_not(borrowing))
        def _():
            kind = mine(codes, [kind for _, kind in jobs])
            params[0] = own_modes(block_ref[0], kind)
            params[1] = own_modes(block_ref[1], kind)

        @pl.when(borrowing)
        def _():
            pltpu.make_async_copy(params, params, params_recv_sem.at[0]).wait()

        symmetric_gains(noise_ref, params[0], params[1], transition_ref, gain_ref, smoother_ref)

        transition = [[transition_ref[row, column] for column in range(3)] for row in range(3)]
        means, predictions = [], []
        for time in range(times):
            landed(inbox, recv_sem.at[time], time * bands, bands)
            arrived = inbox[time * bands : (time + 1) * bands].reshape(bands * ROWS, LANES)
            mixed = paired_dot(forward_lat_ref[...], arrived)
            for hour, spectrum in enumerate(swap_halves(mixed[:n_half], mixed[n_half:]), 2 * time):
                if hour == 0:
                    predictions.append(None)
                    means.append([gain_ref[0, row] * spectrum for row in range(3)])
                    continue
                predicted = mat_vec(transition, means[-1])
                residual = spectrum - predicted[0]
                predictions.append(predicted)
                means.append([predicted[row] + gain_ref[hour, row] * residual for row in range(3)])
        recv_back = recv_back_sem.at[my_job // (KINDS * cosines)]
        smoothed = means[-1]
        series = [None] * hours
        series[hours - 1] = smoothed[0]
        for hour in range(hours - 2, -1, -1):
            difference = [smoothed[row] - predictions[hour + 1][row] for row in range(3)]
            smoothed = [
                means[hour][row]
                + smoother_ref[hour, row, 0] * difference[0]
                + smoother_ref[hour, row, 1] * difference[1]
                + smoother_ref[hour, row, 2] * difference[2]
                for row in range(3)
            ]
            series[hour] = smoothed[0]

        for time in range(times):
            stacked = jnp.concatenate(swap_halves(series[2 * time], series[2 * time + 1]), axis=0)
            grid = paired_dot(inverse_lat_ref[...], stacked)
            boxes_back[time][...] = grid.reshape(bands, ROWS, LANES)
            for other in range(bands - 1, -1, -1):
                copy = exchange(
                    boxes_back[time],
                    inbox_back,
                    send_back_sem,
                    recv_back,
                    peers[other],
                    (time, peers[other]),
                    my_job,
                )
                if other == 0:
                    pl.when(my_time != time)(copy.start)
                else:
                    copy.start()

        for time in range(times):
            pl.when(my_time == time)(keep(boxes_back[time], inbox_back, recv_back, my_band, my_job).start)

    grids = []
    for side in range(2):
        base = side * KINDS * cosines
        landed(inbox_back, recv_back_sem.at[side], base, KINDS * cosines)
        boxes = [
            [inbox_back[base + kind * cosines + local] for local in range(cosines)] for kind in range(KINDS)
        ]
        for parity in range(2):
            blocks = []
            for pair in range(cosines // 2):
                blocks.append(list(swap_halves(*boxes[parity][2 * pair : 2 * pair + 2])))
            shared = []
            for hour in range(2):
                merged = None
                for local in range(cosines):
                    part = spin(boxes[2][local], (local - (2 * hour + parity)) * QUARTER)
                    merged = part if merged is None else jnp.where(quarter == local, part, merged)
                shared.append(merged)
            blocks.append(shared)
            upper, lower = split(
                jnp.concatenate([jnp.concatenate(block, axis=0) for block in blocks], axis=1)
            )
            both = jnp.concatenate([upper, lower], axis=0)
            kind = 2 * side + parity
            wide = lax.dot_general(both, table[kind, 0], NN, preferred_element_type=jnp.float32)
            fine = lax.dot_general(upper, table[kind, 1], NN, preferred_element_type=jnp.float32)
            grids.append(wide[: 2 * ROWS] + wide[2 * ROWS :] + fine)

    origin = inbox_back[KINDS * cosines]
    alternating = jnp.where(lax.rem(lane, 2) == 0, 1.0, -1.0) * math.sqrt(1.0 / lon_size)
    lifted = []
    for hour in range(2):
        value = jnp.broadcast_to(origin[:, hour * WIDTH : hour * WIDTH + 1], (ROWS, LANES)) * alternating
        edge = jnp.where(lane == half // 2 % LANES, 0.5 * value, value)
        lifted.append(jnp.concatenate([value] * (points // LANES - 1) + [edge], axis=1))
    grids[0] = grids[0] + jnp.concatenate(lifted, axis=0)

    count = points // LANES
    for hour in range(2):
        even_cos, odd_cos, even_sin, odd_sin = [grid[hour * ROWS : (hour + 1) * ROWS] for grid in grids]
        ahead, ahead_odd = even_cos + even_sin, odd_cos + odd_sin
        behind, behind_odd = even_cos - even_sin, odd_sin - odd_cos
        for side in range(2):
            start = ahead + ahead_odd if side == 0 else ahead - ahead_odd
            end = behind + behind_odd if side == 0 else behind - behind_odd
            turned = [flipped(tile(end, index)) for index in range(count)]
            pieces = [tile(start, index) for index in range(count - 1)]
            border = half // 2 - (count - 1) * LANES
            fold = tile(start, count - 1)
            fold = jnp.where(lane == border, fold + fold, fold)
            pieces.append(jnp.where(lane <= border, fold, turned[count - 1]))
            for index in range(count - 1, 0, -1):
                pieces.append(jnp.where(straight, turned[index], turned[index - 1]))
            pieces.append(turned[0])
            row = jnp.concatenate(pieces, axis=1)
            out_ref[:, hour, side * half : (side + 1) * half] = row[:lat_dev, :half]

    def gone(box, sends, count):
        left = box.at[pl.ds(0, count), pl.ds(0, lat_dev)]
        pltpu.make_async_copy(left, left, sends.at[0]).wait()

    gone(inbox, send_sem, len(jobs) - 1)

    @pl.when(jnp.logical_not(owning))
    def _():
        gone(inbox, send_sem, 1)

    @pl.when(owning)
    def _():
        gone(inbox, send_back_sem, devices - 1)

    @pl.when(lending)
    def _():
        pltpu.make_async_copy(params_out, params_out, params_send_sem.at[0]).wait()


def per_device_fused(observed, noise_var, spectral_var, time_scale):
    times, bands = lax.axis_size("tm"), lax.axis_size("space")
    hours_dev, lat_dev, lon_size = observed.shape
    hours, lat_size = noise_var.shape[0], spectral_var.shape[1]
    n_half = lat_size // 2
    half_padded = round_up(lon_size // 2, LANES)
    n_jobs = KINDS * bands

    table = lon_tables(lon_size, bands)
    forward_lat, inverse_lat = lat_tables(lat_size, bands)
    in_vmem = pl.BlockSpec(memory_space=pltpu.VMEM)
    in_place = pl.BlockSpec(memory_space=pltpu.HBM)
    box = pltpu.VMEM((times * bands, ROWS, LANES), jnp.float32)
    band_box = pltpu.VMEM((bands, ROWS, LANES), jnp.float32)
    job_box = pltpu.VMEM((n_jobs, ROWS, LANES), jnp.float32)
    dma = pltpu.SemaphoreType.DMA
    field = pl.pallas_call(
        functools.partial(smoother_kernel, times, bands),
        out_shape=pltpu.VMEM((lat_dev, hours_dev, lon_size), jnp.float32),
        in_specs=[in_place] * 7,
        out_specs=in_vmem,
        scratch_shapes=[
            pltpu.VMEM((lat_dev, hours_dev, lon_size), jnp.float32),
            pltpu.SMEM((hours,), jnp.float32),
            pltpu.VMEM((2, lat_size, spectral_var.shape[0]), jnp.float32),
            pltpu.VMEM(forward_lat.shape, jnp.bfloat16),
            pltpu.VMEM(inverse_lat.shape, jnp.bfloat16),
            pltpu.VMEM(table.shape, jnp.bfloat16),
            pltpu.VMEM((2, 2, ROWS, half_padded), jnp.float32),
            box,
            box,
            box,
            band_box,
            band_box,
            band_box,
            band_box,
            job_box,
            pltpu.VMEM((2, n_half, LANES), jnp.float32),
            pltpu.VMEM((2, n_half, LANES), jnp.float32),
            pltpu.VMEM((3, 3, n_half, LANES), jnp.float32),
            pltpu.VMEM((hours, 3, n_half, LANES), jnp.float32),
            pltpu.VMEM((hours, 3, 3, n_half, LANES), jnp.float32),
            dma((5,)),
            dma((4,)),
            dma((1,)),
            dma((times,)),
            dma((1,)),
            dma((2,)),
            dma((1,)),
            dma((1,)),
        ],
        compiler_params=pltpu.CompilerParams(collective_id=0, has_side_effects=True),
    )(
        observed.transpose(1, 0, 2),
        noise_var,
        spectral_var.T,
        time_scale.T,
        jnp.asarray(forward_lat),
        jnp.asarray(inverse_lat),
        jnp.asarray(table),
    )
    return field.transpose(1, 0, 2)


def fits(observed, spectral_var):
    times, bands = lax.axis_size("tm"), lax.axis_size("space")
    hours_dev, lat_dev, lon_size = observed.shape
    modes_dev, lat_size = spectral_var.shape
    full, rest = mode_columns(modes_dev)
    half, points = lon_size // 2, round_up(lon_size // 4 + 1, LANES)
    return (
        hours_dev == 2
        and lat_dev <= ROWS
        and lat_size % (2 * ROWS) == 0
        and times == KINDS + 1
        and balanced(times, bands)
        and 2 * math.isqrt(bands // 2) ** 2 == bands
        and bands == LANES // 16
        and lon_size % 4 == 0
        and modes_dev % 2 == 0
        and modes_dev % KINDS == 0
        and full < WIDTH
        and rest <= QUARTER
        and half % LANES > 0
        and round_up(half, LANES) == 2 * points
        and half // 2 >= points - LANES
    )


def per_device(observed, noise_var, spectral_var, time_scale):
    if fits(observed, spectral_var):
        return per_device_fused(observed, noise_var, spectral_var, time_scale)
    return per_device_general(observed, noise_var, spectral_var, time_scale)


def solution(mesh):
    placed = (P("tm", "space", None), P(), P("space", None), P("space", None))
    return jax.shard_map(
        per_device, mesh=mesh, in_specs=placed, out_specs=P("tm", "space", None), check_vma=False
    )
```

```python
import functools
import math

import jax
import jax.numpy as jnp
import numpy as np
from jax import lax
from jax.experimental import pallas as pl
from jax.experimental.pallas import tpu as pltpu
from jax.sharding import PartitionSpec as P

HIGHEST = lax.Precision.HIGHEST
ROOT_FIVE = 2.23606797749979
NILPOTENT = ((1.0, 1.0, 0.0), (0.0, 1.0, 1.0), (-1.0, -3.0, -2.0))
NILPOTENT_SQUARED = ((1.0, 2.0, 1.0), (-1.0, -2.0, -1.0), (1.0, 2.0, 1.0))
STATIONARY = ((1.0, 0.0, -1.0 / 3.0), (0.0, 1.0 / 3.0, 0.0), (-1.0 / 3.0, 0.0, 1.0))


def lon_basis(size):
    mode_index = lax.broadcasted_iota(jnp.int32, (size, size), 0)
    longitude = lax.broadcasted_iota(jnp.int32, (size, size), 1)
    half_size = size // 2
    sine_rows = mode_index > half_size
    frequency = jnp.where(sine_rows, mode_index - half_size, mode_index)
    radians = (frequency * longitude % size).astype(jnp.float32) * (2.0 * math.pi / size)
    waveform = jnp.where(sine_rows, jnp.sin(radians), jnp.cos(radians))
    edge_rows = (mode_index == 0) | (mode_index == half_size)
    weight = jnp.where(edge_rows, math.sqrt(1.0 / size), math.sqrt(2.0 / size))
    return waveform * weight


def lat_basis(size):
    wavenumber = lax.broadcasted_iota(jnp.int32, (size, size), 0)
    latitude = lax.broadcasted_iota(jnp.int32, (size, size), 1)
    radians = (wavenumber * (2 * latitude + 1) % (4 * size)).astype(jnp.float32) * (
        math.pi / (2.0 * size)
    )
    weight = jnp.where(wavenumber == 0, math.sqrt(1.0 / size), math.sqrt(2.0 / size))
    return jnp.cos(radians) * weight


def mat_mul(left, right):
    return [
        [
            left[across][0] * right[0][within]
            + left[across][1] * right[1][within]
            + left[across][2] * right[2][within]
            for within in range(3)
        ]
        for across in range(3)
    ]


def mat_vec(matrix, vector):
    return [
        matrix[across][0] * vector[0]
        + matrix[across][1] * vector[1]
        + matrix[across][2] * vector[2]
        for across in range(3)
    ]


def transposed(matrix):
    return [[matrix[within][across] for within in range(3)] for across in range(3)]


def inverted(matrix):
    cofactor = [
        [
            matrix[1][1] * matrix[2][2] - matrix[1][2] * matrix[2][1],
            matrix[0][2] * matrix[2][1] - matrix[0][1] * matrix[2][2],
            matrix[0][1] * matrix[1][2] - matrix[0][2] * matrix[1][1],
        ],
        [
            matrix[1][2] * matrix[2][0] - matrix[1][0] * matrix[2][2],
            matrix[0][0] * matrix[2][2] - matrix[0][2] * matrix[2][0],
            matrix[0][2] * matrix[1][0] - matrix[0][0] * matrix[1][2],
        ],
        [
            matrix[1][0] * matrix[2][1] - matrix[1][1] * matrix[2][0],
            matrix[0][1] * matrix[2][0] - matrix[0][0] * matrix[2][1],
            matrix[0][0] * matrix[1][1] - matrix[0][1] * matrix[1][0],
        ],
    ]
    determinant = (
        matrix[0][0] * cofactor[0][0]
        + matrix[0][1] * cofactor[1][0]
        + matrix[0][2] * cofactor[2][0]
    )
    return [[cofactor[across][within] / determinant for within in range(3)] for across in range(3)]


def model_terms(variance, scale):
    decay_rate = ROOT_FIVE / scale
    damping = jnp.exp(-decay_rate)
    transition = [
        [
            damping
            * (
                (1.0 if across == within else 0.0)
                + decay_rate * NILPOTENT[across][within]
                + 0.5 * decay_rate * decay_rate * NILPOTENT_SQUARED[across][within]
            )
            for within in range(3)
        ]
        for across in range(3)
    ]
    stationary = [
        [variance * STATIONARY[across][within] for within in range(3)] for across in range(3)
    ]
    carried = mat_mul(mat_mul(transition, stationary), transposed(transition))
    process_noise = [
        [stationary[across][within] - carried[across][within] for within in range(3)]
        for across in range(3)
    ]
    return (transition, stationary, process_noise)


def predict_cov(covariance, transition, process_noise):
    carried = mat_mul(mat_mul(transition, covariance), transposed(transition))
    return [
        [carried[across][within] + process_noise[across][within] for within in range(3)]
        for across in range(3)
    ]


def gain_and_cov(predicted_cov, noise):
    innovation_var = predicted_cov[0][0] + noise
    kalman_gain = [predicted_cov[across][0] / innovation_var for across in range(3)]
    covariance = [
        [
            predicted_cov[across][within] - kalman_gain[across] * predicted_cov[0][within]
            for within in range(3)
        ]
        for across in range(3)
    ]
    return (kalman_gain, covariance)


def smooth_series(spectra, noise_var, variance, scale):
    transition, stationary, process_noise = model_terms(variance, scale)
    zeros = jnp.zeros_like(variance)

    def forward(carry, inputs):
        mean_state, covariance = carry
        observed, noise = inputs
        predicted_cov = predict_cov(covariance, transition, process_noise)
        smoother_gain = mat_mul(
            mat_mul(covariance, transposed(transition)), inverted(predicted_cov)
        )
        predicted = mat_vec(transition, mean_state)
        kalman_gain, covariance = gain_and_cov(predicted_cov, noise)
        residual = observed - predicted[0]
        mean_state = [predicted[across] + kalman_gain[across] * residual for across in range(3)]
        return ((mean_state, covariance), (mean_state, smoother_gain))

    _, (means, gains) = lax.scan(forward, ([zeros, zeros, zeros], stationary), (spectra, noise_var))

    def backward(later, inputs):
        mean_state, smoother_gain = inputs
        projected = mat_vec(transition, mean_state)
        difference = [later[across] - projected[across] for across in range(3)]
        correction = mat_vec(smoother_gain, difference)
        smoothed_state = [mean_state[across] + correction[across] for across in range(3)]
        return (smoothed_state, smoothed_state[0])

    last_state = [means[across][-1] for across in range(3)]
    earlier_means = [means[across][:-1] for across in range(3)]
    next_gains = [[gains[across][within][1:] for within in range(3)] for across in range(3)]
    _, field = lax.scan(backward, last_state, (earlier_means, next_gains), reverse=True)
    return jnp.concatenate([field, last_state[0][None]], axis=0)


def per_device_general(observed, noise_var, spectral_var, time_scale):
    hours_dev, lat_dev, lon_size = observed.shape
    band_count = lax.axis_size("space")
    lat_size = lat_dev * band_count
    modes_dev = lon_size // band_count
    lon_table = lon_basis(lon_size)
    lat_table = lat_basis(lat_size).reshape(lat_size, band_count, lat_dev)
    grid_rows = observed.reshape(hours_dev * lat_dev, lon_size)
    spectra = lax.dot_general(lon_table, grid_rows, (((1,), (1,)), ((), ())), precision=HIGHEST)
    by_mode = lax.all_to_all(spectra, "space", split_axis=0, concat_axis=1, tiled=True)
    by_mode = by_mode.reshape(modes_dev, band_count, hours_dev, lat_dev)
    coefficients = jnp.einsum("msha,nsa->hmn", by_mode, lat_table, precision=HIGHEST)
    flat = coefficients.reshape(hours_dev, modes_dev * lat_size)
    hourly = lax.all_to_all(flat, "tm", split_axis=1, concat_axis=0, tiled=True)
    share = flat.shape[1] // lax.axis_size("tm")
    offset = lax.axis_index("tm") * share
    variance = lax.dynamic_slice_in_dim(spectral_var.reshape(-1), offset, share)
    scale = lax.dynamic_slice_in_dim(time_scale.reshape(-1), offset, share)
    series = smooth_series(hourly, noise_var, variance, scale)
    smooth = lax.all_to_all(series, "tm", split_axis=0, concat_axis=1, tiled=True).reshape(
        hours_dev, modes_dev, lat_size
    )
    latitude_grid = jnp.einsum("hmn,nsa->msha", smooth, lat_table, precision=HIGHEST)
    latitude_grid = latitude_grid.reshape(modes_dev, band_count * hours_dev * lat_dev)
    by_band = lax.all_to_all(latitude_grid, "space", split_axis=1, concat_axis=0, tiled=True)
    field = lax.dot_general(by_band, lon_table, (((0,), (0,)), ((), ())), precision=HIGHEST)
    return field.reshape(hours_dev, lat_dev, lon_size)


LANES = 128
ROWS = 8
MESH = pl.DeviceIdType.MESH
NT = (((1,), (1,)), ((), ()))
NN = (((1,), (0,)), ((), ()))


def round_up(value, unit):
    return -(-value // unit) * unit


KINDS = 3
WIDTH = LANES // 2
QUARTER = LANES // 4


def hops(time, band, times, bands):
    wide = math.isqrt(bands // 2)
    return time // 2 + band // wide + band % wide


def spare(time, band, bands):
    level = band // math.isqrt(bands // 2)
    return time % 2 == 1 and time // 2 + level == 1


def plan(times, bands):
    cosines = bands // 2
    jobs = [
        (band, kind)
        for base in (0, cosines)
        for kind in range(KINDS)
        for band in range(base, base + cosines)
    ]
    devices = [(time, band) for time in range(times) for band in range(bands)]
    chosen = sorted(devices, key=lambda d: (hops(*d, times, bands), d))[: len(jobs)]
    owner, sources, used = {}, {}, {}
    for band in range(bands):
        local = sorted((d for d in chosen if d[1] == band), key=lambda d: (spare(*d, bands), d))
        for kind, device in enumerate(local[:KINDS]):
            owner[band, kind] = device
    taken = set(owner.values())
    free = sorted((d for d in chosen if d not in taken), key=lambda d: -hops(*d, times, bands))
    for job in jobs:
        if job not in owner:
            owner[job] = free.pop(0)
            sources[job] = (used.get(job[0], 0), job[0])
            used[job[0]] = sources[job][0] + 1
    return jobs, [owner[job] for job in jobs], [sources.get(job) for job in jobs]


def balanced(times, bands):
    every = sorted(hops(time, band, times, bands) for time in range(times) for band in range(bands))
    wanted = KINDS * bands
    lower = max(hops(time, band, times, bands) for time in range(times) for band in range(bands // 2))
    return wanted < len(every) and lower <= every[wanted - 1] < every[wanted]


def mode_columns(modes_dev):
    full = modes_dev // KINDS
    return full, modes_dev // 2 - full


def lon_tables(lon_size, bands):
    half, cosines = lon_size // 2, bands // 2
    modes_dev = lon_size // bands
    full, rest = mode_columns(modes_dev)
    points = lon_size // 4 + 1
    padded = round_up(points, LANES)
    tables = np.zeros((4, cosines * (WIDTH + QUARTER), padded), np.float64)

    def fill(kind, column, mode):
        frequency = mode - half if mode > half else mode
        radians = (frequency * np.arange(points) % lon_size) * (2.0 * math.pi / lon_size)
        wave = np.sin(radians) if mode > half else np.cos(radians)
        wave = wave * math.sqrt((1.0 if mode in (0, half) else 2.0) / lon_size)
        wave[-1] *= 0.5
        tables[kind, column, :points] = wave

    for band in range(bands):
        for parity in range(2):
            kind = 2 * (band // cosines) + parity
            for index in range(full + rest):
                mode = band * modes_dev + 2 * index + parity
                local = band % cosines
                if index < full:
                    column = local * WIDTH + index
                else:
                    column = cosines * WIDTH + local * QUARTER + index - full
                if mode == half:
                    fill(0, WIDTH - 1, mode)
                else:
                    fill(kind, column, mode)
    tables = tables.astype(np.float32)
    high = tables.astype(jnp.bfloat16)
    low = (tables - high.astype(np.float32)).astype(jnp.bfloat16)
    return np.stack([high, low], axis=1)


def lat_tables(lat_size, bands):
    lat_dev = lat_size // bands
    wavenumber = np.arange(lat_size)[:, None]
    latitude = np.arange(lat_size)[None, :]
    radians = (wavenumber * (2 * latitude + 1) % (4 * lat_size)) * (math.pi / (2.0 * lat_size))
    table = np.cos(radians) * np.where(wavenumber == 0, math.sqrt(1.0 / lat_size), math.sqrt(2.0 / lat_size))
    full = np.zeros((lat_size, bands, ROWS), np.float32)
    full[:, :, :lat_dev] = table.reshape(lat_size, bands, lat_dev)
    full = full.reshape(lat_size, bands * ROWS)

    def stacked(array):
        high = array.astype(jnp.bfloat16)
        return np.concatenate([high, (array - high.astype(np.float32)).astype(jnp.bfloat16)], axis=0)

    return stacked(full), stacked(np.ascontiguousarray(full.T))


def split(value):
    high = value.astype(jnp.bfloat16)
    low = (value - high.astype(jnp.float32)).astype(jnp.bfloat16)
    return high, low


def paired_dot(table, value):
    both = jnp.concatenate(split(value), axis=1)
    product = lax.dot_general(table, both, NN, preferred_element_type=jnp.float32)
    rows = table.shape[0] // 2
    return product[:rows, :LANES] + (product[:rows, LANES:] + product[rows:, :LANES])


def swap_halves(first, second):
    left = lax.broadcasted_iota(jnp.int32, first.shape, 1) < LANES // 2
    return (
        jnp.where(left, first, pltpu.roll(second, LANES // 2, 1)),
        jnp.where(left, pltpu.roll(first, LANES // 2, 1), second),
    )


def symmetric_gains(noise_ref, variance, scale, transition_ref, gain_ref, smoother_ref):
    hours = gain_ref.shape[0]
    transition, stationary, process = model_terms(variance, scale)
    pairs = [(0, 0), (0, 1), (0, 2), (1, 1), (1, 2), (2, 2)]
    for row in range(3):
        for column in range(3):
            transition_ref[row, column] = transition[row][column]

    def unpack(packed):
        matrix = [[None] * 3 for _ in range(3)]
        for (row, column), value in zip(pairs, packed):
            matrix[row][column] = matrix[column][row] = value
        return matrix

    def update(predicted, hour):
        inverse_var = 1.0 / (predicted[0][0] + noise_ref[hour])
        gain = [predicted[row][0] * inverse_var for row in range(3)]
        for row in range(3):
            gain_ref[hour, row] = gain[row]
        return [predicted[row][column] - gain[row] * predicted[0][column] for row, column in pairs]

    def step(hour, packed):
        covariance = unpack(packed)
        moved = mat_mul(transition, covariance)
        predicted = unpack(
            [
                moved[row][0] * transition[column][0]
                + moved[row][1] * transition[column][1]
                + moved[row][2] * transition[column][2]
                + process[row][column]
                for row, column in pairs
            ]
        )
        c00 = predicted[1][1] * predicted[2][2] - predicted[1][2] * predicted[1][2]
        c01 = predicted[0][2] * predicted[1][2] - predicted[0][1] * predicted[2][2]
        c02 = predicted[0][1] * predicted[1][2] - predicted[0][2] * predicted[1][1]
        c11 = predicted[0][0] * predicted[2][2] - predicted[0][2] * predicted[0][2]
        c12 = predicted[0][1] * predicted[0][2] - predicted[0][0] * predicted[1][2]
        c22 = predicted[0][0] * predicted[1][1] - predicted[0][1] * predicted[0][1]
        inverse_det = 1.0 / (predicted[0][0] * c00 + predicted[0][1] * c01 + predicted[0][2] * c02)
        cofactors = unpack([c00, c01, c02, c11, c12, c22])
        for row in range(3):
            scaled = [moved[within][row] * inverse_det for within in range(3)]
            for column in range(3):
                smoother_ref[hour - 1, row, column] = (
                    scaled[0] * cofactors[0][column]
                    + scaled[1] * cofactors[1][column]
                    + scaled[2] * cofactors[2][column]
                )
        return tuple(update(predicted, hour))

    first = tuple(update(stationary, 0))
    lax.fori_loop(1, hours, step, first)


def smoother_kernel(
    times,
    bands,
    observed_hbm,
    noise_hbm,
    variance_hbm,
    scale_hbm,
    forward_lat_hbm,
    inverse_lat_hbm,
    table_hbm,
    out_ref,
    observed_ref,
    noise_ref,
    block_ref,
    forward_lat_ref,
    inverse_lat_ref,
    table,
    folded,
    outbox_cos,
    outbox_sin,
    inbox,
    back_0,
    back_1,
    back_2,
    back_3,
    inbox_back,
    params_out,
    params,
    transition_ref,
    gain_ref,
    smoother_ref,
    input_sem,
    table_sem,
    send_sem,
    recv_sem,
    send_back_sem,
    recv_back_sem,
    params_send_sem,
    params_recv_sem,
):
    devices = times * bands
    cosines = bands // 2
    outboxes = (outbox_cos, outbox_sin)
    boxes_back = (back_0, back_1, back_2, back_3)
    jobs, owners, sources = plan(times, bands)
    codes = [time * bands + band for time, band in owners]
    my_time = lax.axis_index("tm")
    my_band = lax.axis_index("space")
    me = my_time * bands + my_band
    lat_dev, lon_size = observed_ref.shape[0], observed_ref.shape[2]
    half = lon_size // 2
    hours = gain_ref.shape[0]
    n_half = gain_ref.shape[2]
    modes_dev = block_ref.shape[2]
    full, rest = mode_columns(modes_dev)
    points = table.shape[3]
    mirror = half % LANES

    def mine(places, values):
        total = 0
        for place, value in zip(places, values):
            total = total + jnp.where(me == place, value, 0)
        return total

    deep = math.isqrt(bands // 2)
    limit = max(hops(*owner, times, bands) for owner in owners)
    row, core = my_time // 2, my_time % 2
    plane, column = my_band // deep, my_band % deep

    def flip(bit, turn):
        return 1 - bit if turn else bit

    rows = [flip(row, turn) for turn in range(2)]
    near, peers = [], []
    for turn in range(bands):
        level = 2 * flip(plane // 2, turn // 4) + flip(plane % 2, turn // 2 % 2)
        across = flip(column, turn % 2)
        near.append(level + across)
        peers.append(level * deep + across)
    owning = row + near[0] <= limit

    def table_copy(kind):
        return pltpu.make_async_copy(table_hbm.at[kind], table.at[kind], table_sem.at[kind])

    inputs = [
        pltpu.make_async_copy(source, target, input_sem.at[index])
        for index, (source, target) in enumerate(
            [
                (observed_hbm, observed_ref),
                (noise_hbm, noise_ref),
                (forward_lat_hbm, forward_lat_ref),
                (inverse_lat_hbm, inverse_lat_ref),
            ]
        )
    ]
    pltpu.make_async_copy(variance_hbm, block_ref.at[0], input_sem.at[4]).start()
    pltpu.make_async_copy(scale_hbm, block_ref.at[1], input_sem.at[4]).start()
    inputs[0].start()
    table_copy(0).start()
    table_copy(1).start()
    table_copy(2).start()
    table_copy(3).start()
    for copy in inputs[1:]:
        copy.start()
    inbox[...] = jnp.zeros_like(inbox)
    inbox_back[...] = jnp.zeros_like(inbox_back)

    barrier = pltpu.get_barrier_semaphore()

    @pl.when(owning)
    def _():
        for turn in range(devices - 1, 0, -1):
            time = 2 * rows[turn // bands // 2] + flip(core, turn // bands % 2)
            pl.semaphore_signal(
                barrier, inc=1, device_id=(time, peers[turn % bands]), device_id_type=MESH
            )

    my_job = mine(codes, range(1, len(jobs) + 1)) - 1
    moved = [index for index, source in enumerate(sources) if source is not None]
    source_codes = [sources[index][0] * bands + sources[index][1] for index in moved]
    lending = mine(source_codes, [1] * len(moved)) > 0
    borrowing = mine([codes[index] for index in moved], [1] * len(moved)) > 0

    def own_modes(kind, target):
        mode = lax.broadcasted_iota(jnp.int32, (modes_dev, LANES), 0)
        slot = lax.rem(lax.broadcasted_iota(jnp.int32, (modes_dev, LANES), 1), WIDTH)
        second = (slot >= QUARTER).astype(jnp.int32)
        place = slot - second * QUARTER
        whole = jnp.where(slot < full, 2 * slot + kind, modes_dev)
        mixed = jnp.where(place < rest, 2 * (full + place) + second, modes_dev)
        wanted = jnp.where(kind == KINDS - 1, mixed, whole)
        picked = (mode == wanted).astype(jnp.float32).astype(jnp.bfloat16)
        lane = lax.broadcasted_iota(jnp.int32, (n_half, LANES), 1)
        used = wanted[:n_half] < modes_dev
        block = block_ref[...].reshape(4 * n_half, modes_dev)
        high = block.astype(jnp.bfloat16)
        left = block - high.astype(jnp.float32)
        parts = jnp.concatenate([high, *split(left)], axis=0)
        value = lax.dot_general(parts, picked, NN, preferred_element_type=jnp.float32)
        value = value[: 4 * n_half] + value[4 * n_half : 8 * n_half] + value[8 * n_half :]
        for index in range(2):
            lower = value[2 * index * n_half : (2 * index + 1) * n_half]
            upper = value[(2 * index + 1) * n_half : (2 * index + 2) * n_half]
            target[index] = jnp.where(used, jnp.where(lane < WIDTH, lower, upper), 1.0)

    folded[...] = jnp.zeros_like(folded)
    pltpu.make_async_copy(block_ref, block_ref, input_sem.at[4]).wait()

    @pl.when(lending)
    def _():
        own_modes(mine(source_codes, [jobs[index][1] for index in moved]), params_out)

    inputs[0].wait()
    lane = lax.broadcasted_iota(jnp.int32, (ROWS, LANES), 1)
    reverse = lax.rem(mirror + LANES - lane, LANES)
    straight = lane <= mirror

    def flipped(value):
        return jnp.take_along_axis(value, reverse, axis=1, mode="promise_in_bounds")

    def tile(value, index):
        return value[:, index * LANES : (index + 1) * LANES]

    last = half // LANES
    classes = [[], [], [], []]
    for hour in range(2):
        early = observed_ref[:, hour, :half]
        late = observed_ref[:, hour, half:]
        folded[0, hour, :lat_dev, :half] = early + late
        folded[1, hour, :lat_dev, :half] = early - late
        for parity in range(2):
            ahead = folded[parity, hour]
            turned = {index: flipped(tile(ahead, index)) for index in range(last - points // LANES, last + 1)}
            behind = jnp.concatenate(
                [
                    jnp.where(straight, turned[last - index], turned[last - index - 1])
                    for index in range(points // LANES)
                ],
                axis=1,
            )
            ahead = ahead[:, :points]
            classes[parity].append(ahead + behind if parity == 0 else ahead - behind)
            classes[2 + parity].append(ahead - behind if parity == 0 else ahead + behind)

    wide_lanes = cosines * WIDTH

    def forward(kind):
        table_copy(kind).wait()
        upper, lower = split(jnp.concatenate(classes[kind], axis=0))
        both = jnp.concatenate([upper, lower], axis=0)
        wide = lax.dot_general(both, table[kind, 0], NT, preferred_element_type=jnp.float32)
        fine = lax.dot_general(upper, table[kind, 1], NT, preferred_element_type=jnp.float32)
        return wide[: 2 * ROWS] + wide[2 * ROWS :] + fine

    def spin(value, amount):
        amount = amount % LANES
        return pltpu.roll(value, amount, 1) if amount else value

    quarter = lane // QUARTER
    middle = None

    def transform(side):
        nonlocal middle
        found = [forward(2 * side), forward(2 * side + 1)]
        base = side * KINDS * cosines
        for parity in range(2):
            for pair in range(cosines // 2):
                block = tile(found[parity], pair)
                first, second = swap_halves(block[:ROWS], block[ROWS:])
                if side == 0 and parity == 0 and pair == 0:
                    middle = spin(first, 1)
                    first = jnp.where(lax.rem(lane, WIDTH) == WIDTH - 1, 0.0, first)
                if side == 1 and parity == 0 and pair == 0:
                    first = jnp.where(lax.rem(lane, WIDTH) == 0, pltpu.roll(middle, WIDTH, 1), first)
                outboxes[side][codes[base + parity * cosines + 2 * pair]] = first
                outboxes[side][codes[base + parity * cosines + 2 * pair + 1]] = second
        mixed = [value[:, wide_lanes:] for value in found]
        for local in range(cosines):
            parts = [
                spin(mixed[part % 2][(part // 2) * ROWS : (part // 2 + 1) * ROWS], (part - local) * QUARTER)
                for part in range(4)
            ]
            merged = jnp.where(quarter == 0, parts[0], parts[1])
            merged = jnp.where(quarter == 2, parts[2], merged)
            outboxes[side][codes[base + 2 * cosines + local]] = jnp.where(quarter == 3, parts[3], merged)

    def params_copy():
        target = mine(source_codes, [codes[index] for index in moved])
        return pltpu.make_async_remote_copy(
            src_ref=params_out,
            dst_ref=params,
            send_sem=params_send_sem.at[0],
            recv_sem=params_recv_sem.at[0],
            device_id=(target // bands, lax.rem(target, bands)),
            device_id_type=MESH,
        )

    def exchange(box, landing, sends, recv, slot, peer, target):
        return pltpu.make_async_remote_copy(
            src_ref=box.at[slot, pl.ds(0, lat_dev)],
            dst_ref=landing.at[target, pl.ds(0, lat_dev)],
            send_sem=sends.at[0],
            recv_sem=recv,
            device_id=peer,
            device_id_type=MESH,
        )

    def keep(box, landing, recv, slot, target):
        return pltpu.make_async_copy(
            box.at[slot, pl.ds(0, lat_dev)], landing.at[target, pl.ds(0, lat_dev)], recv
        )

    def landed(landing, recv, first, count):
        come = landing.at[pl.ds(first, count), pl.ds(0, lat_dev)]
        pltpu.make_async_copy(come, come, recv).wait()

    def forth(box, time, band, wanted):
        @pl.when(wanted)
        def _():
            exchange(
                box, inbox, send_sem, recv_sem.at[my_time], time * bands + band, (time, band), me
            ).start()

    upper_half = plane // 2

    def place(top, turn):
        level = 2 * top + flip(plane % 2, turn // 2)
        across = flip(column, turn % 2)
        return level * deep + across, level + across

    def send(side):
        for turn in range(times - 1, -1, -1):
            next_row, next_core = rows[turn // 2], flip(core, turn % 2)
            for other in range(deep * deep - 1, -1, -1):
                band, height = place(side, other)
                if side == 0:
                    wanted = (next_core == 0) | (next_row + flip(plane % 2, other // 2) != 1)
                else:
                    wanted = next_row + height <= limit
                if turn == 0 and other == 0:
                    wanted = wanted & (upper_half != side)
                forth(outboxes[side], 2 * next_row + next_core, band, wanted)
        if side == 1:
            for other in range(deep * deep - 1, -1, -1):
                band, _ = place(0, other)
                time = 2 * (1 - flip(plane % 2, other // 2)) + 1
                wanted = (my_time != time) | (upper_half != 0) if other == 0 else my_time >= 0
                forth(outboxes[1], time, band, wanted)

    transform(0)
    pl.semaphore_wait(barrier, len(jobs) - owning.astype(jnp.int32))

    @pl.when(lending)
    def _():
        params_copy().start()

    send(0)
    transform(1)
    send(1)

    for copy in inputs[1:]:
        copy.wait()

    @pl.when(owning)
    def _():
        for side in range(2):
            inside = (my_job < KINDS * cosines) == (side == 0)
            pl.when(inside)(keep(outboxes[side], inbox, recv_sem.at[my_time], me, me).start)

        @pl.when(jnp.logical_not(borrowing))
        def _():
            own_modes(mine(codes, [kind for _, kind in jobs]), params)

        @pl.when(borrowing)
        def _():
            pltpu.make_async_copy(params, params, params_recv_sem.at[0]).wait()

        symmetric_gains(noise_ref, params[0], params[1], transition_ref, gain_ref, smoother_ref)

        transition = [[transition_ref[row, column] for column in range(3)] for row in range(3)]
        means, predictions = [], []
        for first in range(0, times, 2):
            spectra = []
            for time in (first, first + 1):
                landed(inbox, recv_sem.at[time], time * bands, bands)
            for time in (first, first + 1):
                arrived = inbox[time * bands : (time + 1) * bands].reshape(bands * ROWS, LANES)
                mixed = paired_dot(forward_lat_ref[...], arrived)
                spectra.extend(swap_halves(mixed[:n_half], mixed[n_half:]))
            for hour, spectrum in enumerate(spectra, 2 * first):
                if hour == 0:
                    predictions.append(None)
                    means.append([gain_ref[0, row] * spectrum for row in range(3)])
                    continue
                predicted = mat_vec(transition, means[-1])
                residual = spectrum - predicted[0]
                predictions.append(predicted)
                means.append([predicted[row] + gain_ref[hour, row] * residual for row in range(3)])
        recv_back = recv_back_sem.at[my_job // (KINDS * cosines)]
        smoothed = means[-1]
        series = [None] * hours
        series[hours - 1] = smoothed[0]
        for hour in range(hours - 2, -1, -1):
            difference = [smoothed[row] - predictions[hour + 1][row] for row in range(3)]
            smoothed = [
                means[hour][row]
                + smoother_ref[hour, row, 0] * difference[0]
                + smoother_ref[hour, row, 1] * difference[1]
                + smoother_ref[hour, row, 2] * difference[2]
                for row in range(3)
            ]
            series[hour] = smoothed[0]

        for time in range(times):
            stacked = jnp.concatenate(swap_halves(series[2 * time], series[2 * time + 1]), axis=0)
            grid = paired_dot(inverse_lat_ref[...], stacked)
            boxes_back[time][...] = grid.reshape(bands, ROWS, LANES)
            for other in range(bands - 1, -1, -1):
                copy = exchange(
                    boxes_back[time],
                    inbox_back,
                    send_back_sem,
                    recv_back,
                    peers[other],
                    (time, peers[other]),
                    my_job,
                )
                if other == 0:
                    pl.when(my_time != time)(copy.start)
                else:
                    copy.start()

        for time in range(times):
            pl.when(my_time == time)(keep(boxes_back[time], inbox_back, recv_back, my_band, my_job).start)

    grids = []
    for side in range(2):
        base = side * KINDS * cosines
        landed(inbox_back, recv_back_sem.at[side], base, KINDS * cosines)
        boxes = [
            [inbox_back[base + kind * cosines + local] for local in range(cosines)] for kind in range(KINDS)
        ]
        for parity in range(2):
            blocks = []
            for pair in range(cosines // 2):
                blocks.append(list(swap_halves(*boxes[parity][2 * pair : 2 * pair + 2])))
            shared = []
            for hour in range(2):
                merged = None
                for local in range(cosines):
                    part = spin(boxes[2][local], (local - (2 * hour + parity)) * QUARTER)
                    merged = part if merged is None else jnp.where(quarter == local, part, merged)
                shared.append(merged)
            blocks.append(shared)
            upper, lower = split(
                jnp.concatenate([jnp.concatenate(block, axis=0) for block in blocks], axis=1)
            )
            both = jnp.concatenate([upper, lower], axis=0)
            kind = 2 * side + parity
            wide = lax.dot_general(both, table[kind, 0], NN, preferred_element_type=jnp.float32)
            fine = lax.dot_general(upper, table[kind, 1], NN, preferred_element_type=jnp.float32)
            grids.append(wide[: 2 * ROWS] + wide[2 * ROWS :] + fine)

    origin = inbox_back[KINDS * cosines]
    alternating = jnp.where(lax.rem(lane, 2) == 0, 1.0, -1.0) * math.sqrt(1.0 / lon_size)
    lifted = []
    for hour in range(2):
        value = jnp.broadcast_to(origin[:, hour * WIDTH : hour * WIDTH + 1], (ROWS, LANES)) * alternating
        edge = jnp.where(lane == half // 2 % LANES, 0.5 * value, value)
        lifted.append(jnp.concatenate([value] * (points // LANES - 1) + [edge], axis=1))
    grids[0] = grids[0] + jnp.concatenate(lifted, axis=0)

    count = points // LANES
    for hour in range(2):
        even_cos, odd_cos, even_sin, odd_sin = [grid[hour * ROWS : (hour + 1) * ROWS] for grid in grids]
        ahead, ahead_odd = even_cos + even_sin, odd_cos + odd_sin
        behind, behind_odd = even_cos - even_sin, odd_sin - odd_cos
        for side in range(2):
            start = ahead + ahead_odd if side == 0 else ahead - ahead_odd
            end = behind + behind_odd if side == 0 else behind - behind_odd
            turned = [flipped(tile(end, index)) for index in range(count)]
            pieces = [tile(start, index) for index in range(count - 1)]
            border = half // 2 - (count - 1) * LANES
            fold = tile(start, count - 1)
            fold = jnp.where(lane == border, fold + fold, fold)
            pieces.append(jnp.where(lane <= border, fold, turned[count - 1]))
            for index in range(count - 1, 0, -1):
                pieces.append(jnp.where(straight, turned[index], turned[index - 1]))
            pieces.append(turned[0])
            row = jnp.concatenate(pieces, axis=1)
            out_ref[:, hour, side * half : (side + 1) * half] = row[:lat_dev, :half]

    def gone(box, sends, count):
        left = box.at[pl.ds(0, count), pl.ds(0, lat_dev)]
        pltpu.make_async_copy(left, left, sends.at[0]).wait()

    gone(inbox, send_sem, len(jobs) - 1)

    @pl.when(jnp.logical_not(owning))
    def _():
        gone(inbox, send_sem, 1)

    @pl.when(owning)
    def _():
        gone(inbox, send_back_sem, devices - 1)

    @pl.when(lending)
    def _():
        pltpu.make_async_copy(params_out, params_out, params_send_sem.at[0]).wait()


def per_device_fused(observed, noise_var, spectral_var, time_scale):
    times, bands = lax.axis_size("tm"), lax.axis_size("space")
    hours_dev, lat_dev, lon_size = observed.shape
    hours, lat_size = noise_var.shape[0], spectral_var.shape[1]
    n_half = lat_size // 2
    half_padded = round_up(lon_size // 2, LANES)
    n_jobs = KINDS * bands

    table = lon_tables(lon_size, bands)
    forward_lat, inverse_lat = lat_tables(lat_size, bands)
    in_vmem = pl.BlockSpec(memory_space=pltpu.VMEM)
    in_place = pl.BlockSpec(memory_space=pltpu.HBM)
    box = pltpu.VMEM((times * bands, ROWS, LANES), jnp.float32)
    band_box = pltpu.VMEM((bands, ROWS, LANES), jnp.float32)
    job_box = pltpu.VMEM((n_jobs, ROWS, LANES), jnp.float32)
    dma = pltpu.SemaphoreType.DMA
    field = pl.pallas_call(
        functools.partial(smoother_kernel, times, bands),
        out_shape=pltpu.VMEM((lat_dev, hours_dev, lon_size), jnp.float32),
        in_specs=[in_place] * 7,
        out_specs=in_vmem,
        scratch_shapes=[
            pltpu.VMEM((lat_dev, hours_dev, lon_size), jnp.float32),
            pltpu.SMEM((hours,), jnp.float32),
            pltpu.VMEM((2, lat_size, spectral_var.shape[0]), jnp.float32),
            pltpu.VMEM(forward_lat.shape, jnp.bfloat16),
            pltpu.VMEM(inverse_lat.shape, jnp.bfloat16),
            pltpu.VMEM(table.shape, jnp.bfloat16),
            pltpu.VMEM((2, 2, ROWS, half_padded), jnp.float32),
            box,
            box,
            box,
            band_box,
            band_box,
            band_box,
            band_box,
            job_box,
            pltpu.VMEM((2, n_half, LANES), jnp.float32),
            pltpu.VMEM((2, n_half, LANES), jnp.float32),
            pltpu.VMEM((3, 3, n_half, LANES), jnp.float32),
            pltpu.VMEM((hours, 3, n_half, LANES), jnp.float32),
            pltpu.VMEM((hours, 3, 3, n_half, LANES), jnp.float32),
            dma((5,)),
            dma((4,)),
            dma((1,)),
            dma((times,)),
            dma((1,)),
            dma((2,)),
            dma((1,)),
            dma((1,)),
        ],
        compiler_params=pltpu.CompilerParams(collective_id=0, has_side_effects=True),
    )(
        observed.transpose(1, 0, 2),
        noise_var,
        spectral_var.T,
        time_scale.T,
        jnp.asarray(forward_lat),
        jnp.asarray(inverse_lat),
        jnp.asarray(table),
    )
    return field.transpose(1, 0, 2)


def fits(observed, spectral_var):
    times, bands = lax.axis_size("tm"), lax.axis_size("space")
    hours_dev, lat_dev, lon_size = observed.shape
    modes_dev, lat_size = spectral_var.shape
    full, rest = mode_columns(modes_dev)
    half, points = lon_size // 2, round_up(lon_size // 4 + 1, LANES)
    return (
        hours_dev == 2
        and lat_dev <= ROWS
        and lat_size % (2 * ROWS) == 0
        and times == KINDS + 1
        and balanced(times, bands)
        and 2 * math.isqrt(bands // 2) ** 2 == bands
        and bands == LANES // 16
        and lon_size % 4 == 0
        and modes_dev % 2 == 0
        and modes_dev % KINDS == 0
        and full < WIDTH
        and rest <= QUARTER
        and half % LANES > 0
        and round_up(half, LANES) == 2 * points
        and half // 2 >= points - LANES
    )


def per_device(observed, noise_var, spectral_var, time_scale):
    if fits(observed, spectral_var):
        return per_device_fused(observed, noise_var, spectral_var, time_scale)
    return per_device_general(observed, noise_var, spectral_var, time_scale)


def solution(mesh):
    placed = (P("tm", "space", None), P(), P("space", None), P("space", None))
    return jax.shard_map(
        per_device, mesh=mesh, in_specs=placed, out_specs=P("tm", "space", None), check_vma=False
    )
```
